128 devices in a mesh: pair: 2 (over core), virt: 64 (over z, y, x).
Axes of the slice: x: 4, y: 4, z: 4, core: 2. Of those that a mesh axis runs over, the one named last changes fastest.
Arguments:
- amplitudes: bfloat16 [512, 32768], P('virt', 'pair'), may hold values from -6 to 6
- integrals: bfloat16 [32768, 32768], P('virt', 'pair'), may hold values from -0.03125 to 0.03125
- cycle_integrals: bfloat16 [16384, 16384], P('pair', 'virt'), may hold values from -0.125 to 0.125
- virt_count: int32 [8], replicated, may hold values from 32 to 64, as said below
Outputs:
- ladder: bfloat16 [512, 32768], P(None, 'virt')
- cycle: bfloat16 [8192, 16384], P('pair', 'virt')
The draws below stay inside these ranges and needn't reach their ends.
Inputs may be any that keep to these rules, and one draw needn't show every extreme that they name: `virt_count`: every irrep keeps at least half of its 64 slots; some irrep has all 64 and some has exactly half.
All inputs are finite; a program needn't handle non-finite values.
Results may differ from the reference program's by a relative error of at most 0.0049.
Values may be sent and summed in bfloat16 or wider, within the bound.
No kernel may reach another device: no remote copies, remote signals or barrier semaphores. Data moves between devices by JAX's collectives and lax.ppermute only.
A program may use at most 256 MiB of HBM per device.

```python
import jax
import jax.numpy as jnp
from jax import lax

VH = 64
IRREPS = 8
OI = 16
OJ = 32
P_SIZE = 512
NAB = 32768
IA = 8192
KC = 16384
JB = 16384


def draw_virt_count(key, part):
    key_order, key_values = jax.random.split(jax.random.fold_in(key, 11))
    order = jax.random.permutation(key_order, IRREPS)
    values = jax.random.randint(key_values, (IRREPS,), VH // 2, VH + 1)
    values = jnp.where(order == 0, VH, jnp.where(order == 1, VH // 2, values))
    return values.astype(jnp.int32)


def level_of(stream_key, shape, cuts, low, high):
    def one(position, parts):
        draws = jax.random.uniform(jax.random.fold_in(jax.random.fold_in(stream_key, 6), position), (parts,), jnp.float32, low / len(cuts), high / len(cuts))
        return jnp.repeat(jnp.exp(draws), shape[position] // parts).reshape((-1,) + (1,) * (len(shape) - position - 1))

    gain = one(*cuts[0])
    for cut in cuts[1:]:
        gain = gain * one(*cut)
    return gain


def noise(stream_key, extent, width, reach, shards=(), kind=jnp.bfloat16):
    factor_of = level_of(stream_key, extent, shards, -0.22, 0.18) if shards else 1.0
    result = jax.random.normal(stream_key, extent, jnp.float32) * width * factor_of
    return jnp.minimum(jnp.maximum(result, -reach), reach).astype(kind)


def setup_inputs(seed: int = 0) -> dict:
    arg_keys = jax.random.split(jax.random.key(seed), 5)
    amplitudes = noise(arg_keys[0], (P_SIZE, NAB), 1.0, 6.0, ((0, 64), (1, 2)))
    integrals = noise(arg_keys[1], (NAB, NAB), NAB ** -0.5, 0.03125, ((0, 64), (1, 2)))
    cycle_integrals = noise(arg_keys[2], (KC, JB), (OJ * VH) ** -0.5, 0.125, ((0, 2), (1, 64)))
    virt_count = draw_virt_count(jax.random.fold_in(arg_keys[4], 71), 0)
    return dict(amplitudes=amplitudes, integrals=integrals, cycle_integrals=cycle_integrals, virt_count=virt_count)


def live_slots(virt_count):
    slot_ids = jnp.arange(VH, dtype=jnp.int32)
    return (slot_ids[None, :] < virt_count[:, None]).astype(jnp.float32)


def reference(amplitudes, integrals, cycle_integrals, virt_count):
    live_slot = live_slots(virt_count)
    pair_live = (live_slot[:, :, None] * live_slot[:, None, :]).reshape(NAB)
    masked = amplitudes * pair_live[None, :].astype(jnp.bfloat16)
    masked_wide = masked.astype(jnp.float32)
    row_blocks = integrals.reshape(IRREPS, NAB // IRREPS, NAB)

    def ladder_block(irrep):
        block_rows = lax.dynamic_index_in_dim(row_blocks, irrep, 0, keepdims=False).astype(jnp.float32)
        return lax.dot_general(masked_wide, block_rows, (((1,), (1,)), ((), ())), precision=lax.Precision.HIGHEST)

    ladder_parts = lax.map(ladder_block, jnp.arange(IRREPS, dtype=jnp.int32))
    summed_ladder = jnp.transpose(ladder_parts, (1, 0, 2)).reshape(P_SIZE, NAB)
    ladder = (summed_ladder * pair_live[None, :]).astype(jnp.bfloat16)
    amp_grid = ladder.astype(jnp.float32).reshape(OI, OJ, IRREPS, VH, VH)
    cycle_blocks = cycle_integrals.reshape(OJ, IRREPS, VH, JB)

    def cycle_block(irrep):
        amp_part = lax.dynamic_index_in_dim(amp_grid, irrep, 2, keepdims=False)
        cycle_part = lax.dynamic_index_in_dim(cycle_blocks, irrep, 1, keepdims=False).astype(jnp.float32)
        return jnp.einsum("ikac,kcj->iaj", amp_part, cycle_part, precision=lax.Precision.HIGHEST)

    cycle_parts = lax.map(cycle_block, jnp.arange(IRREPS, dtype=jnp.int32))
    summed = jnp.transpose(cycle_parts, (1, 0, 2, 3)).reshape(IA, JB)
    keep_cols = jnp.tile(live_slot.reshape(IRREPS * VH), OJ)
    cycle = (summed * keep_cols[None, :]).astype(jnp.bfloat16)
    return ladder, cycle
```

```python
import jax
import jax.numpy as jnp
from jax import lax
from jax.experimental import pallas as pl
from jax.experimental.pallas import tpu as pltpu
from jax.sharding import PartitionSpec as P

VH = 64
OI = 16
OJ = 32
F32 = jnp.float32
BF16 = jnp.bfloat16


def irrep_sizes(virt_count, irrep_of):
    irrep_ids = jnp.arange(virt_count.shape[0], dtype=jnp.int32)
    return jnp.sum(
        jnp.where(irrep_of[:, None] == irrep_ids[None, :], virt_count[None, :], 0), axis=1
    )


def pair_mask(virt_count, first_pos, length, slot_width):
    position = first_pos + jnp.arange(length, dtype=jnp.int32)
    irrep_of = position // (slot_width * slot_width)
    slot_one = position // slot_width % slot_width
    slot_two = position % slot_width
    irrep_size = irrep_sizes(virt_count, irrep_of)
    return ((slot_one < irrep_size) & (slot_two < irrep_size)).astype(F32)


def slot_mask(virt_count, first_pos, length, slot_width):
    position = (first_pos + jnp.arange(length, dtype=jnp.int32)) % (
        virt_count.shape[0] * slot_width
    )
    irrep_of = position // slot_width
    slot_ids = position % slot_width
    return (slot_ids < irrep_sizes(virt_count, irrep_of)).astype(F32)


def combine_kernel(own_ref, other_ref, keep_ref, ladder_ref, turned_ref, rows_ref, turn_ref):
    i_count = 8
    total = (own_ref[...] + other_ref[...]) * keep_ref[...]
    rounded = total.astype(BF16)
    ladder_ref[...] = rounded
    wide = rounded.astype(F32)
    for lane in range(4):
        rows_ref[lane] = wide[:, lane * 128 : (lane + 1) * 128]
    for kk in range(OJ // 2):
        for lane in range(4):
            even = rows_ref[lane, pl.ds(2 * kk, i_count, stride=OJ), :]
            odd = rows_ref[lane, pl.ds(2 * kk + 1, i_count, stride=OJ), :]
            turn_ref[kk, (2 * lane) * 8 : (2 * lane) * 8 + 8, :] = jnp.concatenate(
                [even[:, :VH], odd[:, :VH]], axis=1
            )
            turn_ref[kk, (2 * lane + 1) * 8 : (2 * lane + 1) * 8 + 8, :] = jnp.concatenate(
                [even[:, VH:], odd[:, VH:]], axis=1
            )
    for kk in range(OJ // 2):
        for i in range(i_count):
            turned_ref[i * 8 : (i + 1) * 8, kk * 128 : (kk + 1) * 128] = turn_ref[
                kk, pl.ds(i, 8, stride=8), :
            ].astype(BF16)


def combine(own, other, keep):
    rows, cols = own.shape
    return pl.pallas_call(
        combine_kernel,
        out_shape=(
            jax.ShapeDtypeStruct((rows, cols), BF16),
            jax.ShapeDtypeStruct((rows * cols // (OJ * VH), OJ * VH), BF16),
        ),
        scratch_shapes=[
            pltpu.VMEM((4, rows, 128), F32),
            pltpu.VMEM((OJ // 2, rows * cols // (OJ * VH), 128), F32),
        ],
        cost_estimate=pl.CostEstimate(flops=4 * rows * cols, bytes_accessed=12 * rows * cols, transcendentals=0),
    )(own, other, keep)


def cycle_kernel(half_ref, amp_own_ref, amp_other_ref, int_own_ref, int_other_ref, keep_ref, out_ref):
    rows = amp_own_ref.shape[0] * amp_own_ref.shape[1]
    depth = amp_own_ref.shape[2]
    width = int_own_ref.shape[3]
    total = jnp.dot(
        amp_own_ref[...].reshape(rows, depth), int_own_ref[...].reshape(depth, width),
        preferred_element_type=F32,
    ) + jnp.dot(
        amp_other_ref[...].reshape(rows, depth), int_other_ref[...].reshape(depth, width),
        preferred_element_type=F32,
    )
    total = (total * keep_ref[...]).astype(F32).reshape(8, 8, 8, width)
    for shard in range(8):
        out_ref[:, shard] = total[shard].astype(BF16)


def cycle_sum(half, gathered, int_own, int_other, keep):
    width = int_own.shape[3]
    depth = int_own.shape[0] * int_own.shape[2]
    grid_spec = pltpu.PrefetchScalarGridSpec(
        num_scalar_prefetch=1,
        grid=(8,),
        in_specs=[
            pl.BlockSpec((8, 64, depth), lambda h, half: (h, 0, half[0])),
            pl.BlockSpec((8, 64, depth), lambda h, half: (h, 0, 1 - half[0])),
            pl.BlockSpec((16, 1, 64, width), lambda h, half: (0, h, 0, 0)),
            pl.BlockSpec((16, 1, 64, width), lambda h, half: (0, h, 0, 0)),
            pl.BlockSpec((1, width), lambda h, half: (0, 0)),
        ],
        out_specs=pl.BlockSpec((8, 8, 8, width), lambda h, half: (0, h, 0, 0)),
    )
    return pl.pallas_call(
        cycle_kernel,
        out_shape=jax.ShapeDtypeStruct((8, 64, 8, width), BF16),
        grid_spec=grid_spec,
        compiler_params=pltpu.CompilerParams(
            dimension_semantics=("arbitrary",), vmem_limit_bytes=60 << 20
        ),
        cost_estimate=pl.CostEstimate(
            flops=2 * 4096 * 2048 * 256, bytes_accessed=27 << 20, transcendentals=0
        ),
    )(half, gathered, gathered, int_own, int_other, keep)


def body(amplitudes, integrals, cycle_integrals, virt_count):
    slot_width = VH
    ab_count = integrals.shape[0]
    cd_count = integrals.shape[1]
    jb_count = cycle_integrals.shape[1]
    pair = lax.axis_index("pair")
    virt = lax.axis_index("virt")
    swap = [(0, 1), (1, 0)]
    cycle_other = lax.ppermute(cycle_integrals, "pair", swap)
    masked = amplitudes * pair_mask(virt_count, pair * cd_count, cd_count, slot_width)[
        None, :
    ].astype(BF16)
    partial_sums = lax.dot_general(
        lax.all_gather(masked, "virt", axis=0, tiled=True),
        integrals,
        (((1,), (1,)), ((), ())),
        preferred_element_type=F32,
    )
    keep_pairs = pair_mask(virt_count, virt * ab_count, ab_count, slot_width)[None, :]
    half_rows = partial_sums.shape[0] // 2
    sent = lax.dynamic_slice_in_dim(partial_sums, (1 - pair) * half_rows, half_rows, 0)
    own = lax.dynamic_slice_in_dim(partial_sums, pair * half_rows, half_rows, 0)
    other = lax.ppermute(sent, "pair", swap)
    ladder_own, turned = combine(own, other, keep_pairs)
    gathered = lax.all_gather(turned, "virt", axis=0, tiled=True).reshape(64, 64, OJ * VH)
    ladder_other = lax.ppermute(ladder_own, "pair", swap)
    ladder = jnp.concatenate(
        [
            jnp.where(pair == 0, ladder_own, ladder_other),
            jnp.where(pair == 0, ladder_other, ladder_own),
        ],
        axis=0,
    )
    keep_cols = slot_mask(virt_count, virt * jb_count, jb_count, slot_width)[None, :]
    shape4 = (16, 8, slot_width, jb_count)
    cycle = cycle_sum(
        pair.astype(jnp.int32).reshape(1),
        gathered,
        cycle_integrals.reshape(shape4),
        cycle_other.reshape(shape4),
        keep_cols,
    )
    return (ladder, cycle.reshape(8 * 64 * 8, jb_count))


def solution(mesh):
    placed = (P("virt", "pair"), P("virt", "pair"), P("pair", "virt"), P())
    return jax.shard_map(
        body,
        mesh=mesh,
        in_specs=placed,
        out_specs=(P(None, "virt"), P("pair", "virt")),
        check_vma=False,
    )
```

```python
import jax
import jax.numpy as jnp
from jax import lax
from jax.experimental import pallas as pl
from jax.experimental.pallas import tpu as pltpu
from jax.sharding import PartitionSpec as P

VH = 64
OI = 16
OJ = 32
F32 = jnp.float32
BF16 = jnp.bfloat16


def irrep_sizes(virt_count, irrep_of):
    irrep_ids = jnp.arange(virt_count.shape[0], dtype=jnp.int32)
    return jnp.sum(
        jnp.where(irrep_of[:, None] == irrep_ids[None, :], virt_count[None, :], 0), axis=1
    )


def pair_mask(virt_count, first_pos, length, slot_width):
    position = first_pos + jnp.arange(length, dtype=jnp.int32)
    irrep_of = position // (slot_width * slot_width)
    slot_one = position // slot_width % slot_width
    slot_two = position % slot_width
    irrep_size = irrep_sizes(virt_count, irrep_of)
    return ((slot_one < irrep_size) & (slot_two < irrep_size)).astype(F32)


def slot_mask(virt_count, first_pos, length, slot_width):
    position = (first_pos + jnp.arange(length, dtype=jnp.int32)) % (
        virt_count.shape[0] * slot_width
    )
    irrep_of = position // slot_width
    slot_ids = position % slot_width
    return (slot_ids < irrep_sizes(virt_count, irrep_of)).astype(F32)


SHARDS = 64
SWAP = [(0, 1), (1, 0)]


NT = (((1,), (1,)), ((), ()))
DEPTH = 2048


def ladder_kernel(pair_ref, amp_ref, weight_ref, own_ref, sent_ref, total_ref):
    step = pl.program_id(0)
    part = lax.dot_general(amp_ref[...], weight_ref[...], NT, preferred_element_type=F32)

    @pl.when(step == 0)
    def _():
        total_ref[...] = part

    @pl.when(step > 0)
    def _():
        total_ref[...] += part

    @pl.when(step == pl.num_programs(0) - 1)
    def _():
        half = own_ref.shape[0]
        own_ref[...] = total_ref[pl.ds(pl.multiple_of(pair_ref[0] * half, half), half)]
        sent_ref[...] = total_ref[pl.ds(pl.multiple_of((1 - pair_ref[0]) * half, half), half)]


def ladder_sums(pair, amps, integrals):
    rows, depth = amps.shape
    cols = integrals.shape[0]
    half = jax.ShapeDtypeStruct((rows // 2, cols), F32)
    half_spec = pl.BlockSpec((rows // 2, cols), lambda s, p: (0, 0))
    grid_spec = pltpu.PrefetchScalarGridSpec(
        num_scalar_prefetch=1,
        grid=(depth // DEPTH,),
        in_specs=[
            pl.BlockSpec((rows, DEPTH), lambda s, p: (0, s)),
            pl.BlockSpec((cols, DEPTH), lambda s, p: (0, s)),
        ],
        out_specs=[half_spec, half_spec],
        scratch_shapes=[pltpu.VMEM((rows, cols), F32)],
    )
    return pl.pallas_call(
        ladder_kernel,
        out_shape=[half, half],
        grid_spec=grid_spec,
        compiler_params=pltpu.CompilerParams(
            dimension_semantics=("arbitrary",), vmem_limit_bytes=60 << 20
        ),
        cost_estimate=pl.CostEstimate(
            flops=2 * rows * cols * depth, bytes_accessed=36 << 20, transcendentals=0
        ),
    )(pair, amps, integrals)


def combine_kernel(own_ref, other_ref, keep_ref, ladder_ref, *refs):
    turned_ref, rows_ref, turn_ref = refs
    i_count = 8
    total = (own_ref[...] + other_ref[...]) * keep_ref[...]
    rounded = total.astype(BF16)
    ladder_ref[...] = rounded
    wide = rounded.astype(F32)
    for lane in range(4):
        rows_ref[lane] = wide[:, lane * 128 : (lane + 1) * 128]
    for kk in range(OJ // 2):
        for lane in range(4):
            even = rows_ref[lane, pl.ds(2 * kk, i_count, stride=OJ), :]
            odd = rows_ref[lane, pl.ds(2 * kk + 1, i_count, stride=OJ), :]
            turn_ref[kk, (2 * lane) * 8 : (2 * lane) * 8 + 8, :] = jnp.concatenate(
                [even[:, :VH], odd[:, :VH]], axis=1
            )
            turn_ref[kk, (2 * lane + 1) * 8 : (2 * lane + 1) * 8 + 8, :] = jnp.concatenate(
                [even[:, VH:], odd[:, VH:]], axis=1
            )
    for kk in range(OJ // 2):
        for i in range(i_count):
            turned_ref[i * 8 : i * 8 + 8, kk * 128 : (kk + 1) * 128] = turn_ref[
                kk, pl.ds(i, 8, stride=8), :
            ].astype(BF16)


def combine(own, other, keep):
    rows, cols = own.shape
    return pl.pallas_call(
        combine_kernel,
        out_shape=[jax.ShapeDtypeStruct((rows, cols), BF16)]
        + [jax.ShapeDtypeStruct((64, OJ * VH), BF16)],
        scratch_shapes=[
            pltpu.VMEM((4, rows, 128), F32),
            pltpu.VMEM((OJ // 2, rows * cols // (OJ * VH), 128), F32),
        ],
        cost_estimate=pl.CostEstimate(
            flops=4 * rows * cols, bytes_accessed=12 * rows * cols, transcendentals=0
        ),
    )(own, other, keep)


AHEAD = 2


def fetch_integrals(h, pair, int_own_ref, int_other_ref, int_ref, int_sem):
    for part, source in enumerate((int_own_ref, int_other_ref)):
        first = (pair if part == 0 else 1 - pair) * 16
        pltpu.make_async_copy(
            source.at[:, pl.ds(h, 1)],
            int_ref.at[pl.ds(first, 16), pl.ds(h, 1)],
            int_sem.at[h],
        ).start()


def cycle_kernel(pair_ref, amps_ref, int_own_ref, int_other_ref, keep_ref, out_ref, *scratch):
    amp_ref, int_ref, amp_sem, int_sem = scratch
    keep = keep_ref[...]
    width = keep.shape[1]
    deep = OJ * VH

    def fetch(h):
        fetch_integrals(h, pair_ref[0], int_own_ref, int_other_ref, int_ref, int_sem)
        shards = pl.ds(h * 8, 8)
        pltpu.make_async_copy(amps_ref.at[shards], amp_ref.at[shards], amp_sem.at[h]).start()

    for h in range(AHEAD):
        fetch(h)

    @pl.loop(0, 8)
    def _(h):
        @pl.when(h + AHEAD < 8)
        def _():
            fetch(h + AHEAD)

        ints = int_ref.at[:, pl.ds(h, 1)]
        amps = amp_ref.at[pl.ds(h * 8, 8)]
        pltpu.make_async_copy(ints, ints, int_sem.at[h]).wait()
        pltpu.make_async_copy(amps, amps, amp_sem.at[h]).wait()
        left = amps[...].reshape(8 * 64, deep)
        right = ints[...].reshape(deep, width)
        total = jnp.dot(left, right, preferred_element_type=F32) * keep
        total = total.reshape(8, 8, 8, width)
        for i in range(8):
            out_ref[i, pl.ds(h * 8, 8)] = total[:, i].astype(BF16)


ANYWHERE = pl.BlockSpec(memory_space=pl.ANY)
SCALARS = pl.BlockSpec(memory_space=pltpu.SMEM)
LOCAL = pl.BlockSpec(memory_space=pltpu.VMEM)


def cycle_sum(pair, amps, int_own, int_other, keep):
    width = int_own.shape[3]
    return pl.pallas_call(
        cycle_kernel,
        out_shape=jax.ShapeDtypeStruct((8, SHARDS, 8, width), BF16),
        in_specs=[SCALARS] + [ANYWHERE] * 3 + [LOCAL],
        out_specs=LOCAL,
        scratch_shapes=[
            pltpu.VMEM((SHARDS, 64, OJ * VH), BF16),
            pltpu.VMEM((OJ, 8, VH, width), BF16),
            pltpu.SemaphoreType.DMA((8,)),
            pltpu.SemaphoreType.DMA((8,)),
        ],
        compiler_params=pltpu.CompilerParams(vmem_limit_bytes=60 << 20),
        cost_estimate=pl.CostEstimate(
            flops=2 * 4096 * 2048 * 256, bytes_accessed=27 << 20, transcendentals=0
        ),
    )(pair, amps, int_own, int_other, keep)


def body(amplitudes, integrals, cycle_integrals, virt_count):
    slot_width = VH
    ab_count = integrals.shape[0]
    cd_count = integrals.shape[1]
    jb_count = cycle_integrals.shape[1]
    pair = lax.axis_index("pair")
    virt = lax.axis_index("virt")
    pair_id = pair.astype(jnp.int32).reshape(1)
    cycle_other = lax.ppermute(cycle_integrals, "pair", SWAP)
    masked = amplitudes * pair_mask(virt_count, pair * cd_count, cd_count, slot_width)[
        None, :
    ].astype(BF16)
    amps = lax.all_gather(masked, "virt", axis=0, tiled=True)
    own, sent = ladder_sums(pair_id, amps, integrals)
    keep_pairs = pair_mask(virt_count, virt * ab_count, ab_count, slot_width)[None, :]
    other = lax.ppermute(sent, "pair", SWAP)
    ladder_own, turned = combine(own, other, keep_pairs)
    amps = lax.all_gather(turned, "virt", axis=0, tiled=True).reshape(SHARDS, 64, OJ * VH)
    ladder_other = lax.ppermute(ladder_own, "pair", SWAP)
    ladder = jnp.concatenate(
        [
            jnp.where(pair == 0, ladder_own, ladder_other),
            jnp.where(pair == 0, ladder_other, ladder_own),
        ],
        axis=0,
    )
    keep_cols = slot_mask(virt_count, virt * jb_count, jb_count, slot_width)[None, :]
    shape4 = (16, 8, slot_width, jb_count)
    cycle = cycle_sum(
        pair_id, amps, cycle_integrals.reshape(shape4), cycle_other.reshape(shape4), keep_cols
    )
    return (ladder, cycle.reshape(8 * SHARDS * 8, jb_count))


def solution(mesh):
    placed = (P("virt", "pair"), P("virt", "pair"), P("pair", "virt"), P())
    return jax.shard_map(
        body,
        mesh=mesh,
        in_specs=placed,
        out_specs=(P(None, "virt"), P("pair", "virt")),
        check_vma=False,
    )
```

```python
import jax
import jax.numpy as jnp
from jax import lax
from jax.experimental import pallas as pl
from jax.experimental.pallas import tpu as pltpu
from jax.sharding import PartitionSpec as P

VH = 64
OI = 16
OJ = 32
F32 = jnp.float32
BF16 = jnp.bfloat16


def irrep_sizes(virt_count, irrep_of):
    irrep_ids = jnp.arange(virt_count.shape[0], dtype=jnp.int32)
    return jnp.sum(
        jnp.where(irrep_of[:, None] == irrep_ids[None, :], virt_count[None, :], 0), axis=1
    )


def pair_mask(virt_count, first_pos, length, slot_width):
    position = first_pos + jnp.arange(length, dtype=jnp.int32)
    irrep_of = position // (slot_width * slot_width)
    slot_one = position // slot_width % slot_width
    slot_two = position % slot_width
    irrep_size = irrep_sizes(virt_count, irrep_of)
    return ((slot_one < irrep_size) & (slot_two < irrep_size)).astype(F32)


def slot_mask(virt_count, first_pos, length, slot_width):
    position = (first_pos + jnp.arange(length, dtype=jnp.int32)) % (
        virt_count.shape[0] * slot_width
    )
    irrep_of = position // slot_width
    slot_ids = position % slot_width
    return (slot_ids < irrep_sizes(virt_count, irrep_of)).astype(F32)


SHARDS = 64
SWAP = [(0, 1), (1, 0)]


ANYWHERE = pl.BlockSpec(memory_space=pl.ANY)
SCALARS = pl.BlockSpec(memory_space=pltpu.SMEM)
LOCAL = pl.BlockSpec(memory_space=pltpu.VMEM)


NT = (((1,), (1,)), ((), ()))
DEPTH = 2048


def ladder_kernel(pair_ref, amp_ref, weight_ref, own_ref, sent_ref, total_ref):
    step = pl.program_id(0)
    part = lax.dot_general(amp_ref[...], weight_ref[...], NT, preferred_element_type=F32)

    @pl.when(step == 0)
    def _():
        total_ref[...] = part

    @pl.when(step > 0)
    def _():
        total_ref[...] += part

    @pl.when(step == pl.num_programs(0) - 1)
    def _():
        half = own_ref.shape[0]
        own_ref[...] = total_ref[pl.ds(pl.multiple_of(pair_ref[0] * half, half), half)]
        sent_ref[...] = total_ref[pl.ds(pl.multiple_of((1 - pair_ref[0]) * half, half), half)]


def live_tiles(count):
    return (count * count + 127) // 128


def pack_amps_kernel(count_ref, pair_ref, amp_ref, out_ref, wide_ref, part_ref, all_ref):
    irreps = 4
    tiles = VH * VH // 128
    rows = amp_ref.shape[0]
    lane = lax.broadcasted_iota(jnp.int32, (rows, 128), 1)
    wide_ref[...] = amp_ref[...].astype(F32)
    part_ref[...] = jnp.zeros_like(part_ref)
    counts = [count_ref[pair_ref[0] * irreps + h] for h in range(irreps)]

    @pl.loop(0, VH // 2)
    def _(row):
        todo = []
        for h in range(irreps):
            source = wide_ref[:, pl.ds(pl.multiple_of((h * tiles + row) * 128, 128), 128)]
            for odd in range(2):
                slot = 2 * row + odd
                first = slot * counts[h]
                place = lax.rem(first, 128)
                turned = pltpu.roll(source, lax.rem(place + 128 - VH * odd, 128), 1)
                size = jnp.where(slot < counts[h], counts[h], 0)
                tile = jnp.minimum(first // 128, tiles - 1)
                todo.append((h, tile, place, size, turned))
        for h, tile, place, size, turned in todo:
            here = part_ref.at[h, :, pl.ds(pl.multiple_of(tile * 128, 128), 128)]
            here[...] = jnp.where((lane >= place) & (lane < place + size), turned, here[...])
            after = part_ref.at[h, :, pl.ds(pl.multiple_of(tile * 128 + 128, 128), 128)]
            after[...] = jnp.where(lane < place + size - 128, turned, after[...])

    all_ref[...] = jnp.zeros_like(all_ref)
    tile = jnp.int32(0)
    for h in range(irreps):
        all_ref[:, pl.ds(pl.multiple_of(tile * 128, 128), VH * VH)] = part_ref[h, :, : VH * VH]
        tile += live_tiles(counts[h])
    out_ref[...] = all_ref[:, : out_ref.shape[1]].astype(BF16)


def pack_amps(count, pair, amps):
    rows, cols = amps.shape
    return pl.pallas_call(
        pack_amps_kernel,
        out_shape=jax.ShapeDtypeStruct((rows, cols), BF16),
        in_specs=[SCALARS, SCALARS, LOCAL],
        out_specs=LOCAL,
        scratch_shapes=[
            pltpu.VMEM((rows, cols), F32),
            pltpu.VMEM((4, rows, VH * VH + 128), F32),
            pltpu.VMEM((rows, cols + VH * VH), F32),
        ],
        cost_estimate=pl.CostEstimate(
            flops=32 * rows * cols, bytes_accessed=4 * rows * cols, transcendentals=0
        ),
    )(count, pair, amps)


WINDOW = 6 * VH


def pack_weights_kernel(count_ref, pair_ref, weight_ref, out_ref):
    irreps = 4
    irrep = pl.program_id(0)
    count = count_ref[pair_ref[0] * irreps + irrep]
    first = jnp.int32(0)
    for h in range(irreps - 1):
        first += jnp.where(h < irrep, live_tiles(count_ref[pair_ref[0] * irreps + h]), 0)
    row = lax.broadcasted_iota(jnp.int32, (WINDOW, 128), 0)
    column = lax.broadcasted_iota(jnp.int32, (WINDOW, 128), 1)
    wide_count = count.astype(F32)

    def put(tile, value):
        out_ref[:, pl.ds(pl.multiple_of(tile * 128, 128), 128)] = value

    @pl.loop(0, live_tiles(count))
    def _(tile):
        place = tile * 128 + column
        slot = jnp.floor((place.astype(F32) + 0.5) / wide_count).astype(jnp.int32)
        slot_first = (tile * 128) // count
        base = jnp.minimum(slot_first // 2 * 2, VH - 6)
        found = (slot - base) * VH + place - slot * count
        chosen = ((row == found) & (place < count * count)).astype(F32).astype(BF16)
        window = weight_ref[:, pl.ds(pl.multiple_of(base * VH, 128), WINDOW)]
        put(first + tile, jnp.dot(window, chosen, preferred_element_type=F32).astype(BF16))

    @pl.when(irrep == irreps - 1)
    def _():
        @pl.loop(first + live_tiles(count), out_ref.shape[1] // 128)
        def _(tile):
            put(tile, jnp.zeros((out_ref.shape[0], 128), BF16))


def pack_weights(count, pair, weights):
    rows, cols = weights.shape
    grid_spec = pltpu.PrefetchScalarGridSpec(
        num_scalar_prefetch=2,
        grid=(4,),
        in_specs=[pl.BlockSpec((rows, VH * VH), lambda h, c, p: (0, h))],
        out_specs=pl.BlockSpec((rows, cols), lambda h, c, p: (0, 0)),
    )
    return pl.pallas_call(
        pack_weights_kernel,
        out_shape=jax.ShapeDtypeStruct((rows, cols), BF16),
        grid_spec=grid_spec,
        compiler_params=pltpu.CompilerParams(
            dimension_semantics=("arbitrary",), vmem_limit_bytes=58 << 20
        ),
        cost_estimate=pl.CostEstimate(
            flops=2 * rows * cols * WINDOW, bytes_accessed=4 * rows * cols, transcendentals=0
        ),
    )(count, pair, weights)


def ladder_sums(pair, amps, integrals):
    rows, depth = amps.shape
    cols = integrals.shape[0]
    half = jax.ShapeDtypeStruct((rows // 2, cols), F32)
    half_spec = pl.BlockSpec((rows // 2, cols), lambda s, p: (0, 0))
    grid_spec = pltpu.PrefetchScalarGridSpec(
        num_scalar_prefetch=1,
        grid=(depth // DEPTH,),
        in_specs=[
            pl.BlockSpec((rows, DEPTH), lambda s, p: (0, s)),
            pl.BlockSpec((cols, DEPTH), lambda s, p: (0, s)),
        ],
        out_specs=[half_spec, half_spec],
        scratch_shapes=[pltpu.VMEM((rows, cols), F32)],
    )
    return pl.pallas_call(
        ladder_kernel,
        out_shape=[half, half],
        grid_spec=grid_spec,
        compiler_params=pltpu.CompilerParams(
            dimension_semantics=("arbitrary",), vmem_limit_bytes=60 << 20
        ),
        cost_estimate=pl.CostEstimate(
            flops=2 * rows * cols * depth, bytes_accessed=36 << 20, transcendentals=0
        ),
    )(pair, amps, integrals)


def combine_kernel(own_ref, other_ref, keep_ref, ladder_ref, *refs):
    turned_ref, rows_ref, turn_ref = refs
    i_count = 8
    total = (own_ref[...] + other_ref[...]) * keep_ref[...]
    rounded = total.astype(BF16)
    ladder_ref[...] = rounded
    wide = rounded.astype(F32)
    for lane in range(4):
        rows_ref[lane] = wide[:, lane * 128 : (lane + 1) * 128]
    for kk in range(OJ // 2):
        for lane in range(4):
            even = rows_ref[lane, pl.ds(2 * kk, i_count, stride=OJ), :]
            odd = rows_ref[lane, pl.ds(2 * kk + 1, i_count, stride=OJ), :]
            turn_ref[kk, (2 * lane) * 8 : (2 * lane) * 8 + 8, :] = jnp.concatenate(
                [even[:, :VH], odd[:, :VH]], axis=1
            )
            turn_ref[kk, (2 * lane + 1) * 8 : (2 * lane + 1) * 8 + 8, :] = jnp.concatenate(
                [even[:, VH:], odd[:, VH:]], axis=1
            )
    for kk in range(OJ // 2):
        for i in range(i_count):
            turned_ref[i * 8 : i * 8 + 8, kk * 128 : (kk + 1) * 128] = turn_ref[
                kk, pl.ds(i, 8, stride=8), :
            ].astype(BF16)


def combine(own, other, keep):
    rows, cols = own.shape
    return pl.pallas_call(
        combine_kernel,
        out_shape=[jax.ShapeDtypeStruct((rows, cols), BF16)]
        + [jax.ShapeDtypeStruct((64, OJ * VH), BF16)],
        scratch_shapes=[
            pltpu.VMEM((4, rows, 128), F32),
            pltpu.VMEM((OJ // 2, rows * cols // (OJ * VH), 128), F32),
        ],
        cost_estimate=pl.CostEstimate(
            flops=4 * rows * cols, bytes_accessed=12 * rows * cols, transcendentals=0
        ),
    )(own, other, keep)


AHEAD = 2


def fetch_integrals(h, pair, int_own_ref, int_other_ref, int_ref, int_sem):
    for part, source in enumerate((int_own_ref, int_other_ref)):
        first = (pair if part == 0 else 1 - pair) * 16
        pltpu.make_async_copy(
            source.at[:, pl.ds(h, 1)],
            int_ref.at[pl.ds(first, 16), pl.ds(h, 1)],
            int_sem.at[h],
        ).start()


def cycle_kernel(pair_ref, amps_ref, int_own_ref, int_other_ref, keep_ref, out_ref, *scratch):
    amp_ref, int_ref, amp_sem, int_sem = scratch
    keep = keep_ref[...]
    width = keep.shape[1]
    deep = OJ * VH

    def fetch(h):
        fetch_integrals(h, pair_ref[0], int_own_ref, int_other_ref, int_ref, int_sem)
        shards = pl.ds(h * 8, 8)
        pltpu.make_async_copy(amps_ref.at[shards], amp_ref.at[shards], amp_sem.at[h]).start()

    for h in range(AHEAD):
        fetch(h)

    @pl.loop(0, 8)
    def _(h):
        @pl.when(h + AHEAD < 8)
        def _():
            fetch(h + AHEAD)

        ints = int_ref.at[:, pl.ds(h, 1)]
        amps = amp_ref.at[pl.ds(h * 8, 8)]
        pltpu.make_async_copy(ints, ints, int_sem.at[h]).wait()
        pltpu.make_async_copy(amps, amps, amp_sem.at[h]).wait()
        left = amps[...].reshape(8 * 64, deep)
        right = ints[...].reshape(deep, width)
        total = jnp.dot(left, right, preferred_element_type=F32) * keep
        total = total.reshape(8, 8, 8, width)
        for i in range(8):
            out_ref[i, pl.ds(h * 8, 8)] = total[:, i].astype(BF16)


def cycle_sum(pair, amps, int_own, int_other, keep):
    width = int_own.shape[3]
    return pl.pallas_call(
        cycle_kernel,
        out_shape=jax.ShapeDtypeStruct((8, SHARDS, 8, width), BF16),
        in_specs=[SCALARS] + [ANYWHERE] * 3 + [LOCAL],
        out_specs=LOCAL,
        scratch_shapes=[
            pltpu.VMEM((SHARDS, 64, OJ * VH), BF16),
            pltpu.VMEM((OJ, 8, VH, width), BF16),
            pltpu.SemaphoreType.DMA((8,)),
            pltpu.SemaphoreType.DMA((8,)),
        ],
        compiler_params=pltpu.CompilerParams(vmem_limit_bytes=60 << 20),
        cost_estimate=pl.CostEstimate(
            flops=2 * 4096 * 2048 * 256, bytes_accessed=27 << 20, transcendentals=0
        ),
    )(pair, amps, int_own, int_other, keep)


def body(amplitudes, integrals, cycle_integrals, virt_count):
    slot_width = VH
    ab_count = integrals.shape[0]
    cd_count = integrals.shape[1]
    jb_count = cycle_integrals.shape[1]
    pair = lax.axis_index("pair")
    virt = lax.axis_index("virt")
    pair_id = pair.astype(jnp.int32).reshape(1)
    cycle_other = lax.ppermute(cycle_integrals, "pair", SWAP)
    packed = pack_amps(virt_count, pair_id, amplitudes)
    widths = [cd_count * n // 8 for n in range(4, 9)]

    def ladder_of(width):
        def sums(count, packed, integrals):
            amps = lax.all_gather(packed[:, :width], "virt", axis=0, tiled=True)
            weights = pack_weights(count, pair_id, integrals)
            return ladder_sums(pair_id, amps, weights)

        return sums

    tiles = live_tiles(virt_count).reshape(2, -1).sum(axis=1).max()
    choice = sum((tiles * 128 > width).astype(jnp.int32) for width in widths[:-1])
    own, sent = lax.switch(
        choice, [ladder_of(width) for width in widths], virt_count, packed, integrals
    )
    keep_pairs = pair_mask(virt_count, virt * ab_count, ab_count, slot_width)[None, :]
    other = lax.ppermute(sent, "pair", SWAP)
    ladder_own, turned = combine(own, other, keep_pairs)
    amps = lax.all_gather(turned, "virt", axis=0, tiled=True).reshape(SHARDS, 64, OJ * VH)
    ladder_other = lax.ppermute(ladder_own, "pair", SWAP)
    ladder = jnp.concatenate(
        [
            jnp.where(pair == 0, ladder_own, ladder_other),
            jnp.where(pair == 0, ladder_other, ladder_own),
        ],
        axis=0,
    )
    keep_cols = slot_mask(virt_count, virt * jb_count, jb_count, slot_width)[None, :]
    shape4 = (16, 8, slot_width, jb_count)
    cycle = cycle_sum(
        pair_id, amps, cycle_integrals.reshape(shape4), cycle_other.reshape(shape4), keep_cols
    )
    return (ladder, cycle.reshape(8 * SHARDS * 8, jb_count))


def solution(mesh):
    placed = (P("virt", "pair"), P("virt", "pair"), P("pair", "virt"), P())
    return jax.shard_map(
        body,
        mesh=mesh,
        in_specs=placed,
        out_specs=(P(None, "virt"), P("pair", "virt")),
        check_vma=False,
    )
```

```python
import jax
import jax.numpy as jnp
from jax import lax
from jax.experimental import pallas as pl
from jax.experimental.pallas import tpu as pltpu
from jax.sharding import PartitionSpec as P

VH = 64
OI = 16
OJ = 32
F32 = jnp.float32
BF16 = jnp.bfloat16


def irrep_sizes(virt_count, irrep_of):
    irrep_ids = jnp.arange(virt_count.shape[0], dtype=jnp.int32)
    return jnp.sum(
        jnp.where(irrep_of[:, None] == irrep_ids[None, :], virt_count[None, :], 0), axis=1
    )


def pair_mask(virt_count, first_pos, length, slot_width):
    position = first_pos + jnp.arange(length, dtype=jnp.int32)
    irrep_of = position // (slot_width * slot_width)
    slot_one = position // slot_width % slot_width
    slot_two = position % slot_width
    irrep_size = irrep_sizes(virt_count, irrep_of)
    return ((slot_one < irrep_size) & (slot_two < irrep_size)).astype(F32)


def slot_mask(virt_count, first_pos, length, slot_width):
    position = (first_pos + jnp.arange(length, dtype=jnp.int32)) % (
        virt_count.shape[0] * slot_width
    )
    irrep_of = position // slot_width
    slot_ids = position % slot_width
    return (slot_ids < irrep_sizes(virt_count, irrep_of)).astype(F32)


SHARDS = 64
SWAP = [(0, 1), (1, 0)]


ANYWHERE = pl.BlockSpec(memory_space=pl.ANY)
SCALARS = pl.BlockSpec(memory_space=pltpu.SMEM)
LOCAL = pl.BlockSpec(memory_space=pltpu.VMEM)


NT = (((1,), (1,)), ((), ()))
STEPS = 8


def ladder_kernel(pair_ref, amp_ref, weight_ref, own_ref, sent_ref, total_ref):
    step = pl.program_id(0)
    part = lax.dot_general(amp_ref[...], weight_ref[...], NT, preferred_element_type=F32)

    @pl.when(step == 0)
    def _():
        total_ref[...] = part

    @pl.when(step > 0)
    def _():
        total_ref[...] += part

    @pl.when(step == pl.num_programs(0) - 1)
    def _():
        half = own_ref.shape[0]
        own_ref[...] = total_ref[pl.ds(pl.multiple_of(pair_ref[0] * half, half), half)]
        sent_ref[...] = total_ref[pl.ds(pl.multiple_of((1 - pair_ref[0]) * half, half), half)]


def live_tiles(count):
    return (count * count + 127) // 128


def pack_amps_kernel(count_ref, pair_ref, amp_ref, out_ref, wide_ref, all_ref, *part_refs):
    irreps = 4
    tiles = VH * VH // 128
    rows = amp_ref.shape[0]
    lane = lax.broadcasted_iota(jnp.int32, (rows, 128), 1)
    wide_ref[...] = amp_ref[...].astype(F32)
    for part_ref in part_refs:
        part_ref[...] = jnp.zeros_like(part_ref)
    counts = [count_ref[pair_ref[0] * irreps + h] for h in range(irreps)]

    @pl.loop(0, VH // 2)
    def _(row):
        todo = []
        for h in range(irreps):
            source = wide_ref[:, pl.ds(pl.multiple_of((h * tiles + row) * 128, 128), 128)]
            for odd in range(2):
                slot = 2 * row + odd
                first = slot * counts[h]
                place = lax.rem(first, 128)
                turned = pltpu.roll(source, lax.rem(place + 128 - VH * odd, 128), 1)
                size = jnp.where(slot < counts[h], counts[h], 0)
                tile = jnp.minimum(first // 128, tiles - 1)
                todo.append((h, tile, place, size, turned))
        for h, tile, place, size, turned in todo:
            here = part_refs[h].at[:, pl.ds(pl.multiple_of(tile * 128, 128), 128)]
            here[...] = jnp.where((lane >= place) & (lane < place + size), turned, here[...])
            after = part_refs[h].at[:, pl.ds(pl.multiple_of(tile * 128 + 128, 128), 128)]
            after[...] = jnp.where(lane < place + size - 128, turned, after[...])

    all_ref[...] = jnp.zeros_like(all_ref)
    tile = jnp.int32(0)
    for h in range(irreps):
        all_ref[:, pl.ds(pl.multiple_of(tile * 128, 128), VH * VH)] = part_refs[h][:, : VH * VH]
        tile += live_tiles(counts[h])
    out_ref[...] = all_ref[:, : out_ref.shape[1]].astype(BF16)


def pack_amps(count, pair, amps, width):
    rows, cols = amps.shape
    return pl.pallas_call(
        pack_amps_kernel,
        out_shape=jax.ShapeDtypeStruct((rows, width), BF16),
        in_specs=[SCALARS, SCALARS, LOCAL],
        out_specs=LOCAL,
        scratch_shapes=[
            pltpu.VMEM((rows, cols), F32),
            pltpu.VMEM((rows, cols + VH * VH), F32),
        ]
        + [pltpu.VMEM((rows, VH * VH + 128), F32)] * 4,
        cost_estimate=pl.CostEstimate(
            flops=32 * rows * cols, bytes_accessed=4 * rows * cols, transcendentals=0
        ),
    )(count, pair, amps)


WINDOW = 6 * VH


def pack_weights_kernel(count_ref, pair_ref, weight_ref, out_ref):
    irreps = 4
    irrep = pl.program_id(0)
    count = count_ref[pair_ref[0] * irreps + irrep]
    first = jnp.int32(0)
    for h in range(irreps - 1):
        first += jnp.where(h < irrep, live_tiles(count_ref[pair_ref[0] * irreps + h]), 0)
    row = lax.broadcasted_iota(jnp.int32, (WINDOW, 128), 0)
    column = lax.broadcasted_iota(jnp.int32, (WINDOW, 128), 1)
    wide_count = count.astype(F32)

    def put(tile, value):
        out_ref[:, pl.ds(pl.multiple_of(tile * 128, 128), 128)] = value

    @pl.loop(0, live_tiles(count))
    def _(tile):
        place = tile * 128 + column
        slot = jnp.floor((place.astype(F32) + 0.5) / wide_count).astype(jnp.int32)
        slot_first = (tile * 128) // count
        base = jnp.minimum(slot_first // 2 * 2, VH - 6)
        found = (slot - base) * VH + place - slot * count
        chosen = ((row == found) & (place < count * count)).astype(F32).astype(BF16)
        window = weight_ref[:, pl.ds(pl.multiple_of(base * VH, 128), WINDOW)]
        put(first + tile, jnp.dot(window, chosen, preferred_element_type=F32).astype(BF16))

    @pl.when(irrep == irreps - 1)
    def _():
        @pl.loop(first + live_tiles(count), out_ref.shape[1] // 128)
        def _(tile):
            put(tile, jnp.zeros((out_ref.shape[0], 128), BF16))


def pack_weights(count, pair, weights, width):
    rows, cols = weights.shape
    grid_spec = pltpu.PrefetchScalarGridSpec(
        num_scalar_prefetch=2,
        grid=(4,),
        in_specs=[pl.BlockSpec((rows, VH * VH), lambda h, c, p: (0, h))],
        out_specs=pl.BlockSpec((rows, width), lambda h, c, p: (0, 0)),
    )
    return pl.pallas_call(
        pack_weights_kernel,
        out_shape=jax.ShapeDtypeStruct((rows, width), BF16),
        grid_spec=grid_spec,
        compiler_params=pltpu.CompilerParams(
            dimension_semantics=("arbitrary",), vmem_limit_bytes=58 << 20
        ),
        cost_estimate=pl.CostEstimate(
            flops=2 * rows * cols * WINDOW, bytes_accessed=4 * rows * cols, transcendentals=0
        ),
    )(count, pair, weights)


def ladder_sums(pair, amps, integrals):
    rows, depth = amps.shape
    cols = integrals.shape[0]
    half = jax.ShapeDtypeStruct((rows // 2, cols), F32)
    half_spec = pl.BlockSpec((rows // 2, cols), lambda s, p: (0, 0))
    grid_spec = pltpu.PrefetchScalarGridSpec(
        num_scalar_prefetch=1,
        grid=(STEPS,),
        in_specs=[
            pl.BlockSpec((rows, depth // STEPS), lambda s, p: (0, s)),
            pl.BlockSpec((cols, depth // STEPS), lambda s, p: (0, s)),
        ],
        out_specs=[half_spec, half_spec],
        scratch_shapes=[pltpu.VMEM((rows, cols), F32)],
    )
    return pl.pallas_call(
        ladder_kernel,
        out_shape=[half, half],
        grid_spec=grid_spec,
        compiler_params=pltpu.CompilerParams(
            dimension_semantics=("arbitrary",), vmem_limit_bytes=60 << 20
        ),
        cost_estimate=pl.CostEstimate(
            flops=2 * rows * cols * depth, bytes_accessed=36 << 20, transcendentals=0
        ),
    )(pair, amps, integrals)


def combine_kernel(own_ref, other_ref, keep_ref, ladder_ref, *refs):
    turned_ref, rows_ref, turn_ref = refs
    i_count = 8
    total = (own_ref[...] + other_ref[...]) * keep_ref[...]
    rounded = total.astype(BF16)
    ladder_ref[...] = rounded
    wide = rounded.astype(F32)
    for lane in range(4):
        rows_ref[lane] = wide[:, lane * 128 : (lane + 1) * 128]
    for kk in range(OJ // 2):
        for lane in range(4):
            even = rows_ref[lane, pl.ds(2 * kk, i_count, stride=OJ), :]
            odd = rows_ref[lane, pl.ds(2 * kk + 1, i_count, stride=OJ), :]
            turn_ref[kk, (2 * lane) * 8 : (2 * lane) * 8 + 8, :] = jnp.concatenate(
                [even[:, :VH], odd[:, :VH]], axis=1
            )
            turn_ref[kk, (2 * lane + 1) * 8 : (2 * lane + 1) * 8 + 8, :] = jnp.concatenate(
                [even[:, VH:], odd[:, VH:]], axis=1
            )
    for kk in range(OJ // 2):
        for i in range(i_count):
            turned_ref[i * 8 : i * 8 + 8, kk * 128 : (kk + 1) * 128] = turn_ref[
                kk, pl.ds(i, 8, stride=8), :
            ].astype(BF16)


def combine(own, other, keep):
    rows, cols = own.shape
    return pl.pallas_call(
        combine_kernel,
        out_shape=[jax.ShapeDtypeStruct((rows, cols), BF16)]
        + [jax.ShapeDtypeStruct((64, OJ * VH), BF16)],
        in_specs=[LOCAL] * 3,
        out_specs=[LOCAL] * 2,
        scratch_shapes=[
            pltpu.VMEM((4, rows, 128), F32),
            pltpu.VMEM((OJ // 2, rows * cols // (OJ * VH), 128), F32),
        ],
        cost_estimate=pl.CostEstimate(
            flops=4 * rows * cols, bytes_accessed=12 * rows * cols, transcendentals=0
        ),
    )(own, other, keep)


AHEAD = 2


def fetch_integrals(h, pair, int_own_ref, int_other_ref, int_ref, int_sem):
    for part, source in enumerate((int_own_ref, int_other_ref)):
        first = (pair if part == 0 else 1 - pair) * 16
        pltpu.make_async_copy(
            source.at[:, pl.ds(h, 1)],
            int_ref.at[pl.ds(first, 16), pl.ds(h, 1)],
            int_sem.at[h],
        ).start()


def cycle_kernel(pair_ref, amps_ref, int_own_ref, int_other_ref, keep_ref, out_ref, *scratch):
    amp_ref, int_ref, made_ref, amp_sem, int_sem, out_sem = scratch
    keep = keep_ref[...]
    width = keep.shape[1]
    deep = OJ * VH

    def fetch(h):
        fetch_integrals(h, pair_ref[0], int_own_ref, int_other_ref, int_ref, int_sem)
        shards = pl.ds(h * 8, 8)
        pltpu.make_async_copy(amps_ref.at[shards], amp_ref.at[shards], amp_sem.at[h]).start()

    for h in range(AHEAD):
        fetch(h)

    @pl.loop(0, 8)
    def _(h):
        @pl.when(h + AHEAD < 8)
        def _():
            fetch(h + AHEAD)

        ints = int_ref.at[:, pl.ds(h, 1)]
        amps = amp_ref.at[pl.ds(h * 8, 8)]
        pltpu.make_async_copy(ints, ints, int_sem.at[h]).wait()
        pltpu.make_async_copy(amps, amps, amp_sem.at[h]).wait()
        left = amps[...].reshape(8 * 64, deep)
        right = ints[...].reshape(deep, width)
        total = jnp.dot(left, right, preferred_element_type=F32) * keep
        total = total.reshape(8, 8, 8, width)
        for i in range(8):
            made_ref[i, pl.ds(h * 8, 8)] = total[:, i].astype(BF16)
        shards = pl.ds(h * 8, 8)
        pltpu.make_async_copy(made_ref.at[:, shards], out_ref.at[:, shards], out_sem).start()

    pltpu.make_async_copy(made_ref, out_ref, out_sem).wait()


def cycle_sum(pair, amps, int_own, int_other, keep):
    width = int_own.shape[3]
    return pl.pallas_call(
        cycle_kernel,
        out_shape=jax.ShapeDtypeStruct((8, SHARDS, 8, width), BF16),
        in_specs=[SCALARS] + [ANYWHERE] * 3 + [LOCAL],
        out_specs=ANYWHERE,
        scratch_shapes=[
            pltpu.VMEM((SHARDS, 64, OJ * VH), BF16),
            pltpu.VMEM((OJ, 8, VH, width), BF16),
            pltpu.VMEM((8, SHARDS, 8, width), BF16),
            pltpu.SemaphoreType.DMA((8,)),
            pltpu.SemaphoreType.DMA((8,)),
            pltpu.SemaphoreType.DMA,
        ],
        compiler_params=pltpu.CompilerParams(vmem_limit_bytes=60 << 20),
        cost_estimate=pl.CostEstimate(
            flops=2 * 4096 * 2048 * 256, bytes_accessed=27 << 20, transcendentals=0
        ),
    )(pair, amps, int_own, int_other, keep)


def body(amplitudes, integrals, cycle_integrals, virt_count):
    slot_width = VH
    ab_count = integrals.shape[0]
    cd_count = integrals.shape[1]
    jb_count = cycle_integrals.shape[1]
    pair = lax.axis_index("pair")
    virt = lax.axis_index("virt")
    pair_id = pair.astype(jnp.int32).reshape(1)
    cycle_other = lax.ppermute(cycle_integrals, "pair", SWAP)
    widths = [cd_count * n // 16 for n in range(7, 17)]

    def ladder_of(width):
        def sums(count, amplitudes, integrals):
            packed = pack_amps(count, pair_id, amplitudes, width)
            amps = lax.all_gather(packed, "virt", axis=0, tiled=True)
            weights = pack_weights(count, pair_id, integrals, width)
            return ladder_sums(pair_id, amps, weights)

        return sums

    tiles = live_tiles(virt_count).reshape(2, -1).sum(axis=1).max()
    choice = sum((tiles * 128 > width).astype(jnp.int32) for width in widths[:-1])
    own, sent = lax.switch(
        choice, [ladder_of(width) for width in widths], virt_count, amplitudes, integrals
    )
    keep_pairs = pair_mask(virt_count, virt * ab_count, ab_count, slot_width)[None, :]
    other = lax.ppermute(sent, "pair", SWAP)
    ladder_own, turned = combine(own, other, keep_pairs)
    amps = lax.all_gather(turned, "virt", axis=0, tiled=True).reshape(SHARDS, 64, OJ * VH)
    ladder_other = lax.ppermute(ladder_own, "pair", SWAP)
    ladder = jnp.concatenate(
        [
            jnp.where(pair == 0, ladder_own, ladder_other),
            jnp.where(pair == 0, ladder_other, ladder_own),
        ],
        axis=0,
    )
    keep_cols = slot_mask(virt_count, virt * jb_count, jb_count, slot_width)[None, :]
    shape4 = (16, 8, slot_width, jb_count)
    cycle = cycle_sum(
        pair_id, amps, cycle_integrals.reshape(shape4), cycle_other.reshape(shape4), keep_cols
    )
    return (ladder, cycle.reshape(8 * SHARDS * 8, jb_count))


def solution(mesh):
    placed = (P("virt", "pair"), P("virt", "pair"), P("pair", "virt"), P())
    return jax.shard_map(
        body,
        mesh=mesh,
        in_specs=placed,
        out_specs=(P(None, "virt"), P("pair", "virt")),
        check_vma=False,
    )
```

```python
import jax
import jax.numpy as jnp
from jax import lax
from jax.experimental import pallas as pl
from jax.experimental.pallas import tpu as pltpu
from jax.sharding import PartitionSpec as P

VH = 64
OI = 16
OJ = 32
F32 = jnp.float32
BF16 = jnp.bfloat16


def irrep_sizes(virt_count, irrep_of):
    irrep_ids = jnp.arange(virt_count.shape[0], dtype=jnp.int32)
    return jnp.sum(
        jnp.where(irrep_of[:, None] == irrep_ids[None, :], virt_count[None, :], 0), axis=1
    )


def pair_mask(virt_count, first_pos, length, slot_width):
    position = first_pos + jnp.arange(length, dtype=jnp.int32)
    irrep_of = position // (slot_width * slot_width)
    slot_one = position // slot_width % slot_width
    slot_two = position % slot_width
    irrep_size = irrep_sizes(virt_count, irrep_of)
    return ((slot_one < irrep_size) & (slot_two < irrep_size)).astype(F32)


def slot_mask(virt_count, first_pos, length, slot_width):
    position = (first_pos + jnp.arange(length, dtype=jnp.int32)) % (
        virt_count.shape[0] * slot_width
    )
    irrep_of = position // slot_width
    slot_ids = position % slot_width
    return (slot_ids < irrep_sizes(virt_count, irrep_of)).astype(F32)


SHARDS = 64
SWAP = [(0, 1), (1, 0)]


ANYWHERE = pl.BlockSpec(memory_space=pl.ANY)
SCALARS = pl.BlockSpec(memory_space=pltpu.SMEM)
LOCAL = pl.BlockSpec(memory_space=pltpu.VMEM)


NT = (((1,), (1,)), ((), ()))
STEPS = 8


def ladder_kernel(
    pair_ref, amp_ref, weight_ref, own_ref, sent_ref, held_ref, held_weight_ref, total_ref, sems
):
    depth = held_ref.shape[1] // STEPS

    def part(step):
        return pl.ds(pl.multiple_of(step * depth, 128), depth)

    def fetches(step):
        return [
            pltpu.make_async_copy(source.at[:, part(step)], held.at[:, part(step)], sems.at[n, step])
            for n, (source, held) in enumerate(((amp_ref, held_ref), (weight_ref, held_weight_ref)))
        ]

    for step in range(STEPS):
        for copy in fetches(step):
            copy.start()
    total_ref[...] = jnp.zeros_like(total_ref)

    @pl.loop(0, STEPS)
    def _(step):
        for copy in fetches(step):
            copy.wait()
        total_ref[...] += lax.dot_general(
            held_ref[:, part(step)], held_weight_ref[:, part(step)], NT, preferred_element_type=F32
        )

    half = own_ref.shape[0]
    own_ref[...] = total_ref[pl.ds(pl.multiple_of(pair_ref[0] * half, half), half)]
    sent_ref[...] = total_ref[pl.ds(pl.multiple_of((1 - pair_ref[0]) * half, half), half)]


def live_tiles(count):
    return (count * count + 127) // 128


def pack_amps_kernel(count_ref, pair_ref, amp_ref, out_ref, wide_ref, all_ref, *part_refs):
    irreps = 4
    tiles = VH * VH // 128
    rows = amp_ref.shape[0]
    lane = lax.broadcasted_iota(jnp.int32, (rows, 128), 1)
    wide_ref[...] = amp_ref[...].astype(F32)
    for part_ref in part_refs:
        part_ref[...] = jnp.zeros_like(part_ref)
    counts = [count_ref[pair_ref[0] * irreps + h] for h in range(irreps)]

    @pl.loop(0, VH // 2)
    def _(row):
        todo = []
        for h in range(irreps):
            source = wide_ref[:, pl.ds(pl.multiple_of((h * tiles + row) * 128, 128), 128)]
            for odd in range(2):
                slot = 2 * row + odd
                first = slot * counts[h]
                place = lax.rem(first, 128)
                turned = pltpu.roll(source, lax.rem(place + 128 - VH * odd, 128), 1)
                size = jnp.where(slot < counts[h], counts[h], 0)
                tile = jnp.minimum(first // 128, tiles - 1)
                todo.append((h, tile, place, size, turned))
        for h, tile, place, size, turned in todo:
            here = part_refs[h].at[:, pl.ds(pl.multiple_of(tile * 128, 128), 128)]
            here[...] = jnp.where((lane >= place) & (lane < place + size), turned, here[...])
            after = part_refs[h].at[:, pl.ds(pl.multiple_of(tile * 128 + 128, 128), 128)]
            after[...] = jnp.where(lane < place + size - 128, turned, after[...])

    all_ref[...] = jnp.zeros_like(all_ref)
    tile = jnp.int32(0)
    for h in range(irreps):
        all_ref[:, pl.ds(pl.multiple_of(tile * 128, 128), VH * VH)] = part_refs[h][:, : VH * VH]
        tile += live_tiles(counts[h])
    out_ref[...] = all_ref[:, : out_ref.shape[1]].astype(BF16)


def pack_amps(count, pair, amps, width):
    rows, cols = amps.shape
    return pl.pallas_call(
        pack_amps_kernel,
        out_shape=jax.ShapeDtypeStruct((rows, width), BF16),
        in_specs=[SCALARS, SCALARS, LOCAL],
        out_specs=LOCAL,
        scratch_shapes=[
            pltpu.VMEM((rows, cols), F32),
            pltpu.VMEM((rows, cols + VH * VH), F32),
        ]
        + [pltpu.VMEM((rows, VH * VH + 128), F32)] * 4,
        cost_estimate=pl.CostEstimate(
            flops=32 * rows * cols, bytes_accessed=4 * rows * cols, transcendentals=0
        ),
    )(count, pair, amps)


WINDOW = 6 * VH


def pack_weights_kernel(count_ref, pair_ref, weight_ref, out_ref):
    irreps = 4
    irrep = pl.program_id(0)
    count = count_ref[pair_ref[0] * irreps + irrep]
    first = jnp.int32(0)
    for h in range(irreps - 1):
        first += jnp.where(h < irrep, live_tiles(count_ref[pair_ref[0] * irreps + h]), 0)
    row = lax.broadcasted_iota(jnp.int32, (WINDOW, 128), 0)
    column = lax.broadcasted_iota(jnp.int32, (WINDOW, 128), 1)
    wide_count = count.astype(F32)

    def put(tile, value):
        out_ref[:, pl.ds(pl.multiple_of(tile * 128, 128), 128)] = value

    @pl.loop(0, live_tiles(count))
    def _(tile):
        place = tile * 128 + column
        slot = jnp.floor((place.astype(F32) + 0.5) / wide_count).astype(jnp.int32)
        slot_first = (tile * 128) // count
        base = jnp.minimum(slot_first // 2 * 2, VH - 6)
        found = (slot - base) * VH + place - slot * count
        chosen = ((row == found) & (place < count * count)).astype(F32).astype(BF16)
        window = weight_ref[:, pl.ds(pl.multiple_of(base * VH, 128), WINDOW)]
        put(first + tile, jnp.dot(window, chosen, preferred_element_type=F32).astype(BF16))

    @pl.when(irrep == irreps - 1)
    def _():
        @pl.loop(first + live_tiles(count), out_ref.shape[1] // 128)
        def _(tile):
            put(tile, jnp.zeros((out_ref.shape[0], 128), BF16))


def pack_weights(count, pair, weights, width):
    rows, cols = weights.shape
    grid_spec = pltpu.PrefetchScalarGridSpec(
        num_scalar_prefetch=2,
        grid=(4,),
        in_specs=[pl.BlockSpec((rows, VH * VH), lambda h, c, p: (0, h))],
        out_specs=pl.BlockSpec((rows, width), lambda h, c, p: (0, 0)),
    )
    return pl.pallas_call(
        pack_weights_kernel,
        out_shape=jax.ShapeDtypeStruct((rows, width), BF16),
        grid_spec=grid_spec,
        compiler_params=pltpu.CompilerParams(
            dimension_semantics=("arbitrary",), vmem_limit_bytes=58 << 20
        ),
        cost_estimate=pl.CostEstimate(
            flops=2 * rows * cols * WINDOW, bytes_accessed=4 * rows * cols, transcendentals=0
        ),
    )(count, pair, weights)


def ladder_sums(pair, amps, integrals):
    rows, depth = amps.shape
    cols = integrals.shape[0]
    half = jax.ShapeDtypeStruct((rows // 2, cols), F32)
    return pl.pallas_call(
        ladder_kernel,
        out_shape=[half, half],
        in_specs=[SCALARS, ANYWHERE, ANYWHERE],
        out_specs=[LOCAL, LOCAL],
        scratch_shapes=[
            pltpu.VMEM((rows, depth), BF16),
            pltpu.VMEM((cols, depth), BF16),
            pltpu.VMEM((rows, cols), F32),
            pltpu.SemaphoreType.DMA((2, STEPS)),
        ],
        compiler_params=pltpu.CompilerParams(vmem_limit_bytes=60 << 20),
        cost_estimate=pl.CostEstimate(
            flops=2 * rows * cols * depth, bytes_accessed=36 << 20, transcendentals=0
        ),
    )(pair, amps, integrals)


def combine_kernel(own_ref, other_ref, keep_ref, ladder_ref, *refs):
    turned_ref, rows_ref, turn_ref = refs
    i_count = 8
    total = (own_ref[...] + other_ref[...]) * keep_ref[...]
    rounded = total.astype(BF16)
    ladder_ref[...] = rounded
    wide = rounded.astype(F32)
    for lane in range(4):
        rows_ref[lane] = wide[:, lane * 128 : (lane + 1) * 128]
    for kk in range(OJ // 2):
        for lane in range(4):
            even = rows_ref[lane, pl.ds(2 * kk, i_count, stride=OJ), :]
            odd = rows_ref[lane, pl.ds(2 * kk + 1, i_count, stride=OJ), :]
            turn_ref[kk, (2 * lane) * 8 : (2 * lane) * 8 + 8, :] = jnp.concatenate(
                [even[:, :VH], odd[:, :VH]], axis=1
            )
            turn_ref[kk, (2 * lane + 1) * 8 : (2 * lane + 1) * 8 + 8, :] = jnp.concatenate(
                [even[:, VH:], odd[:, VH:]], axis=1
            )
    for kk in range(OJ // 2):
        for i in range(i_count):
            turned_ref[i * 8 : i * 8 + 8, kk * 128 : (kk + 1) * 128] = turn_ref[
                kk, pl.ds(i, 8, stride=8), :
            ].astype(BF16)


def combine(own, other, keep):
    rows, cols = own.shape
    return pl.pallas_call(
        combine_kernel,
        out_shape=[jax.ShapeDtypeStruct((rows, cols), BF16)]
        + [jax.ShapeDtypeStruct((64, OJ * VH), BF16)],
        in_specs=[LOCAL] * 3,
        out_specs=[LOCAL] * 2,
        scratch_shapes=[
            pltpu.VMEM((4, rows, 128), F32),
            pltpu.VMEM((OJ // 2, rows * cols // (OJ * VH), 128), F32),
        ],
        compiler_params=pltpu.CompilerParams(vmem_limit_bytes=8 << 20),
        cost_estimate=pl.CostEstimate(
            flops=4 * rows * cols, bytes_accessed=12 * rows * cols, transcendentals=0
        ),
    )(own, other, keep)


AHEAD = 2


def fetch_integrals(h, pair, int_own_ref, int_other_ref, int_ref, int_sem):
    for part, source in enumerate((int_own_ref, int_other_ref)):
        first = (pair if part == 0 else 1 - pair) * 16
        pltpu.make_async_copy(
            source.at[:, pl.ds(h, 1)],
            int_ref.at[pl.ds(first, 16), pl.ds(h, 1)],
            int_sem.at[h],
        ).start()


def cycle_kernel(pair_ref, amps_ref, int_own_ref, int_other_ref, keep_ref, out_ref, *scratch):
    amp_ref, int_ref, made_ref, amp_sem, int_sem, out_sem = scratch
    keep = keep_ref[...]
    width = keep.shape[1]
    deep = OJ * VH

    def fetch(h):
        fetch_integrals(h, pair_ref[0], int_own_ref, int_other_ref, int_ref, int_sem)
        shards = pl.ds(h * 8, 8)
        pltpu.make_async_copy(amps_ref.at[shards], amp_ref.at[shards], amp_sem.at[h]).start()

    for h in range(AHEAD):
        fetch(h)

    @pl.loop(0, 8)
    def _(h):
        @pl.when(h + AHEAD < 8)
        def _():
            fetch(h + AHEAD)

        ints = int_ref.at[:, pl.ds(h, 1)]
        amps = amp_ref.at[pl.ds(h * 8, 8)]
        pltpu.make_async_copy(ints, ints, int_sem.at[h]).wait()
        pltpu.make_async_copy(amps, amps, amp_sem.at[h]).wait()
        left = amps[...].reshape(8 * 64, deep)
        right = ints[...].reshape(deep, width)
        total = jnp.dot(left, right, preferred_element_type=F32) * keep
        total = total.reshape(8, 8, 8, width)
        for i in range(8):
            made_ref[i, pl.ds(h * 8, 8)] = total[:, i].astype(BF16)
        shards = pl.ds(h * 8, 8)
        pltpu.make_async_copy(made_ref.at[:, shards], out_ref.at[:, shards], out_sem).start()

    pltpu.make_async_copy(made_ref, out_ref, out_sem).wait()


def cycle_sum(pair, amps, int_own, int_other, keep):
    width = int_own.shape[3]
    return pl.pallas_call(
        cycle_kernel,
        out_shape=jax.ShapeDtypeStruct((8, SHARDS, 8, width), BF16),
        in_specs=[SCALARS] + [ANYWHERE] * 3 + [LOCAL],
        out_specs=ANYWHERE,
        scratch_shapes=[
            pltpu.VMEM((SHARDS, 64, OJ * VH), BF16),
            pltpu.VMEM((OJ, 8, VH, width), BF16),
            pltpu.VMEM((8, SHARDS, 8, width), BF16),
            pltpu.SemaphoreType.DMA((8,)),
            pltpu.SemaphoreType.DMA((8,)),
            pltpu.SemaphoreType.DMA,
        ],
        compiler_params=pltpu.CompilerParams(vmem_limit_bytes=60 << 20),
        cost_estimate=pl.CostEstimate(
            flops=2 * 4096 * 2048 * 256, bytes_accessed=27 << 20, transcendentals=0
        ),
    )(pair, amps, int_own, int_other, keep)


def body(amplitudes, integrals, cycle_integrals, virt_count):
    slot_width = VH
    ab_count = integrals.shape[0]
    cd_count = integrals.shape[1]
    jb_count = cycle_integrals.shape[1]
    pair = lax.axis_index("pair")
    virt = lax.axis_index("virt")
    pair_id = pair.astype(jnp.int32).reshape(1)
    cycle_other = lax.ppermute(cycle_integrals, "pair", SWAP)
    widths = [cd_count * n // 16 for n in range(7, 17)]

    def ladder_of(width):
        def sums(count, amplitudes, integrals):
            packed = pack_amps(count, pair_id, amplitudes, width)
            amps = lax.all_gather(packed, "virt", axis=0, tiled=True)
            weights = pack_weights(count, pair_id, integrals, width)
            return ladder_sums(pair_id, amps, weights)

        return sums

    tiles = live_tiles(virt_count).reshape(2, -1).sum(axis=1).max()
    choice = sum((tiles * 128 > width).astype(jnp.int32) for width in widths[:-1])
    own, sent = lax.switch(
        choice, [ladder_of(width) for width in widths], virt_count, amplitudes, integrals
    )
    keep_pairs = pair_mask(virt_count, virt * ab_count, ab_count, slot_width)[None, :]
    other = lax.ppermute(sent, "pair", SWAP)
    ladder_own, turned = combine(own, other, keep_pairs)
    amps = lax.all_gather(turned, "virt", axis=0, tiled=True).reshape(SHARDS, 64, OJ * VH)
    ladder_other = lax.ppermute(ladder_own, "pair", SWAP)
    ladder = jnp.concatenate(
        [
            jnp.where(pair == 0, ladder_own, ladder_other),
            jnp.where(pair == 0, ladder_other, ladder_own),
        ],
        axis=0,
    )
    keep_cols = slot_mask(virt_count, virt * jb_count, jb_count, slot_width)[None, :]
    shape4 = (16, 8, slot_width, jb_count)
    cycle = cycle_sum(
        pair_id, amps, cycle_integrals.reshape(shape4), cycle_other.reshape(shape4), keep_cols
    )
    return (ladder, cycle.reshape(8 * SHARDS * 8, jb_count))


def solution(mesh):
    placed = (P("virt", "pair"), P("virt", "pair"), P("pair", "virt"), P())
    return jax.shard_map(
        body,
        mesh=mesh,
        in_specs=placed,
        out_specs=(P(None, "virt"), P("pair", "virt")),
        check_vma=False,
    )
```

```python
import jax
import jax.numpy as jnp
from jax import lax
from jax.experimental import pallas as pl
from jax.experimental.pallas import tpu as pltpu
from jax.sharding import PartitionSpec as P

VH = 64
OI = 16
OJ = 32
F32 = jnp.float32
BF16 = jnp.bfloat16


def irrep_sizes(virt_count, irrep_of):
    irrep_ids = jnp.arange(virt_count.shape[0], dtype=jnp.int32)
    return jnp.sum(
        jnp.where(irrep_of[:, None] == irrep_ids[None, :], virt_count[None, :], 0), axis=1
    )


def pair_mask(virt_count, first_pos, length, slot_width):
    position = first_pos + jnp.arange(length, dtype=jnp.int32)
    irrep_of = position // (slot_width * slot_width)
    slot_one = position // slot_width % slot_width
    slot_two = position % slot_width
    irrep_size = irrep_sizes(virt_count, irrep_of)
    return ((slot_one < irrep_size) & (slot_two < irrep_size)).astype(F32)


def slot_mask(virt_count, first_pos, length, slot_width):
    position = (first_pos + jnp.arange(length, dtype=jnp.int32)) % (
        virt_count.shape[0] * slot_width
    )
    irrep_of = position // slot_width
    slot_ids = position % slot_width
    return (slot_ids < irrep_sizes(virt_count, irrep_of)).astype(F32)


SHARDS = 64
SWAP = [(0, 1), (1, 0)]


ANYWHERE = pl.BlockSpec(memory_space=pl.ANY)
SCALARS = pl.BlockSpec(memory_space=pltpu.SMEM)
LOCAL = pl.BlockSpec(memory_space=pltpu.VMEM)


NT = (((1,), (1,)), ((), ()))
STEPS = 8


def ladder_kernel(
    pair_ref, amp_ref, weight_ref, own_ref, sent_ref, held_ref, held_weight_ref, total_ref, sems
):
    depth = held_ref.shape[1] // STEPS

    def part(step):
        return pl.ds(pl.multiple_of(step * depth, 128), depth)

    def fetches(step):
        return [
            pltpu.make_async_copy(source.at[:, part(step)], held.at[:, part(step)], sems.at[n, step])
            for n, (source, held) in enumerate(((amp_ref, held_ref), (weight_ref, held_weight_ref)))
        ]

    for step in range(STEPS):
        for copy in fetches(step):
            copy.start()
    total_ref[...] = jnp.zeros_like(total_ref)

    @pl.loop(0, STEPS)
    def _(step):
        for copy in fetches(step):
            copy.wait()
        total_ref[...] += lax.dot_general(
            held_ref[:, part(step)], held_weight_ref[:, part(step)], NT, preferred_element_type=F32
        )

    half = own_ref.shape[0]
    own_ref[...] = total_ref[pl.ds(pl.multiple_of(pair_ref[0] * half, half), half)]
    sent_ref[...] = total_ref[pl.ds(pl.multiple_of((1 - pair_ref[0]) * half, half), half)]


def live_tiles(count):
    return (count * count + 127) >> 7


def pack_amps_kernel(count_ref, pair_ref, amp_ref, out_ref, wide_ref, all_ref, *part_refs):
    irreps = 4
    tiles = VH * VH // 128
    rows = amp_ref.shape[0]
    lane = lax.broadcasted_iota(jnp.int32, (rows, 128), 1)
    wide_ref[...] = amp_ref[...].astype(F32)
    for part_ref in part_refs:
        part_ref[...] = jnp.zeros_like(part_ref)
    counts = [count_ref[pair_ref[0] * irreps + h] for h in range(irreps)]

    @pl.loop(0, VH // 2, unroll=4)
    def _(row):
        todo = []
        for h in range(irreps):
            source = wide_ref[:, pl.ds(pl.multiple_of((h * tiles + row) * 128, 128), 128)]
            for odd in range(2):
                slot = 2 * row + odd
                first = slot * counts[h]
                place = lax.rem(first, 128)
                turned = pltpu.roll(source, lax.rem(place + 128 - VH * odd, 128), 1)
                size = jnp.where(slot < counts[h], counts[h], 0)
                tile = jnp.minimum(first // 128, tiles - 1)
                todo.append((h, tile, place, size, turned))
        for h, tile, place, size, turned in todo:
            here = part_refs[h].at[:, pl.ds(pl.multiple_of(tile * 128, 128), 128)]
            here[...] = jnp.where((lane >= place) & (lane < place + size), turned, here[...])
            after = part_refs[h].at[:, pl.ds(pl.multiple_of(tile * 128 + 128, 128), 128)]
            after[...] = jnp.where(lane < place + size - 128, turned, after[...])

    all_ref[...] = jnp.zeros_like(all_ref)
    tile = jnp.int32(0)
    for h in range(irreps):
        all_ref[:, pl.ds(pl.multiple_of(tile * 128, 128), VH * VH)] = part_refs[h][:, : VH * VH]
        tile += live_tiles(counts[h])
    out_ref[...] = all_ref[:, : out_ref.shape[1]].astype(BF16)


def pack_amps(count, pair, amps, width):
    rows, cols = amps.shape
    return pl.pallas_call(
        pack_amps_kernel,
        out_shape=jax.ShapeDtypeStruct((rows, width), BF16),
        in_specs=[SCALARS, SCALARS, LOCAL],
        out_specs=LOCAL,
        scratch_shapes=[
            pltpu.VMEM((rows, cols), F32),
            pltpu.VMEM((rows, cols + VH * VH), F32),
        ]
        + [pltpu.VMEM((rows, VH * VH + 128), F32)] * 4,
        cost_estimate=pl.CostEstimate(
            flops=32 * rows * cols, bytes_accessed=4 * rows * cols, transcendentals=0
        ),
    )(count, pair, amps)


WINDOW = 6 * VH


def pack_weights_kernel(count_ref, pair_ref, weight_ref, out_ref):
    irreps = 4
    irrep = pl.program_id(0)
    count = count_ref[pair_ref[0] * irreps + irrep]
    first = jnp.int32(0)
    for h in range(irreps - 1):
        first += jnp.where(h < irrep, live_tiles(count_ref[pair_ref[0] * irreps + h]), 0)
    row = lax.broadcasted_iota(jnp.int32, (WINDOW, 128), 0)
    column = lax.broadcasted_iota(jnp.int32, (WINDOW, 128), 1)
    wide_count = count.astype(F32)

    def put(tile, value):
        out_ref[:, pl.ds(pl.multiple_of(tile * 128, 128), 128)] = value

    @pl.loop(0, live_tiles(count))
    def _(tile):
        place = tile * 128 + column
        slot = jnp.floor((place.astype(F32) + 0.5) / wide_count).astype(jnp.int32)
        slot_first = (tile * 128) // count
        base = jnp.minimum(slot_first // 2 * 2, VH - 6)
        found = (slot - base) * VH + place - slot * count
        chosen = ((row == found) & (place < count * count)).astype(F32).astype(BF16)
        window = weight_ref[:, pl.ds(pl.multiple_of(base * VH, 128), WINDOW)]
        put(first + tile, jnp.dot(window, chosen, preferred_element_type=F32).astype(BF16))

    @pl.when(irrep == irreps - 1)
    def _():
        @pl.loop(first + live_tiles(count), out_ref.shape[1] // 128)
        def _(tile):
            put(tile, jnp.zeros((out_ref.shape[0], 128), BF16))


def pack_weights(count, pair, weights, width):
    rows, cols = weights.shape
    grid_spec = pltpu.PrefetchScalarGridSpec(
        num_scalar_prefetch=2,
        grid=(4,),
        in_specs=[pl.BlockSpec((rows, VH * VH), lambda h, c, p: (0, h))],
        out_specs=pl.BlockSpec((rows, width), lambda h, c, p: (0, 0)),
    )
    return pl.pallas_call(
        pack_weights_kernel,
        out_shape=jax.ShapeDtypeStruct((rows, width), BF16),
        grid_spec=grid_spec,
        compiler_params=pltpu.CompilerParams(
            dimension_semantics=("arbitrary",), vmem_limit_bytes=58 << 20
        ),
        cost_estimate=pl.CostEstimate(
            flops=2 * rows * cols * WINDOW, bytes_accessed=4 * rows * cols, transcendentals=0
        ),
    )(count, pair, weights)


def ladder_sums(pair, amps, integrals):
    rows, depth = amps.shape
    cols = integrals.shape[0]
    half = jax.ShapeDtypeStruct((rows // 2, cols), F32)
    return pl.pallas_call(
        ladder_kernel,
        out_shape=[half, half],
        in_specs=[SCALARS, ANYWHERE, ANYWHERE],
        out_specs=[LOCAL, LOCAL],
        scratch_shapes=[
            pltpu.VMEM((rows, depth), BF16),
            pltpu.VMEM((cols, depth), BF16),
            pltpu.VMEM((rows, cols), F32),
            pltpu.SemaphoreType.DMA((2, STEPS)),
        ],
        compiler_params=pltpu.CompilerParams(vmem_limit_bytes=60 << 20),
        cost_estimate=pl.CostEstimate(
            flops=2 * rows * cols * depth, bytes_accessed=36 << 20, transcendentals=0
        ),
    )(pair, amps, integrals)


def combine_kernel(own_ref, other_ref, keep_ref, ladder_ref, *refs):
    turned_ref, rows_ref, turn_ref = refs
    i_count = 8
    total = (own_ref[...] + other_ref[...]) * keep_ref[...]
    rounded = total.astype(BF16)
    ladder_ref[...] = rounded
    wide = rounded.astype(F32)
    for lane in range(4):
        rows_ref[lane] = wide[:, lane * 128 : (lane + 1) * 128]
    for kk in range(OJ // 2):
        for lane in range(4):
            even = rows_ref[lane, pl.ds(2 * kk, i_count, stride=OJ), :]
            odd = rows_ref[lane, pl.ds(2 * kk + 1, i_count, stride=OJ), :]
            turn_ref[kk, (2 * lane) * 8 : (2 * lane) * 8 + 8, :] = jnp.concatenate(
                [even[:, :VH], odd[:, :VH]], axis=1
            )
            turn_ref[kk, (2 * lane + 1) * 8 : (2 * lane + 1) * 8 + 8, :] = jnp.concatenate(
                [even[:, VH:], odd[:, VH:]], axis=1
            )
    for kk in range(OJ // 2):
        for i in range(i_count):
            turned_ref[i * 8 : i * 8 + 8, kk * 128 : (kk + 1) * 128] = turn_ref[
                kk, pl.ds(i, 8, stride=8), :
            ].astype(BF16)


def combine(own, other, keep):
    rows, cols = own.shape
    return pl.pallas_call(
        combine_kernel,
        out_shape=[jax.ShapeDtypeStruct((rows, cols), BF16)]
        + [jax.ShapeDtypeStruct((64, OJ * VH), BF16)],
        in_specs=[LOCAL] * 3,
        out_specs=[LOCAL] * 2,
        scratch_shapes=[
            pltpu.VMEM((4, rows, 128), F32),
            pltpu.VMEM((OJ // 2, rows * cols // (OJ * VH), 128), F32),
        ],
        compiler_params=pltpu.CompilerParams(vmem_limit_bytes=8 << 20),
        cost_estimate=pl.CostEstimate(
            flops=4 * rows * cols, bytes_accessed=12 * rows * cols, transcendentals=0
        ),
    )(own, other, keep)


def fetch_integrals(h, pair, int_own_ref, int_other_ref, int_ref, int_sem):
    for part, source in enumerate((int_own_ref, int_other_ref)):
        first = (pair if part == 0 else 1 - pair) * 16
        pltpu.make_async_copy(
            source.at[:, pl.ds(h, 1)],
            int_ref.at[pl.ds(first, 16), pl.ds(h, 1)],
            int_sem.at[h],
        ).start()


def cycle_kernel(count_ref, pair_ref, amps_ref, int_own_ref, int_other_ref, keep_ref, out_ref, *scratch):
    amp_ref, int_ref, made_ref, amp_sem, int_sem, out_sem = scratch
    keep = keep_ref[...]
    width = keep.shape[1]
    deep = OJ * VH

    def live_shards(h):
        return jnp.clip((count_ref[h] + 7) >> 3, 4, 8)

    def amps_copy(h, do):
        live = live_shards(h)
        for size in range(4, 9):

            @pl.when(live == size)
            def _(size=size):
                shards = pl.ds(h * 8, size)
                do(pltpu.make_async_copy(amps_ref.at[shards], amp_ref.at[shards], amp_sem.at[h]))

    def fetch(h):
        fetch_integrals(h, pair_ref[0], int_own_ref, int_other_ref, int_ref, int_sem)
        amps_copy(h, lambda copy: copy.start())

    row = lax.broadcasted_iota(jnp.int32, (8 * 64, width), 0)
    @pl.loop(0, 8)
    def _(h):
        fetch(h)

    @pl.loop(0, 8)
    def _(h):
        ints = int_ref.at[:, pl.ds(h, 1)]
        amps = amp_ref.at[pl.ds(h * 8, 8)]
        pltpu.make_async_copy(ints, ints, int_sem.at[h]).wait()
        amps_copy(h, lambda copy: copy.wait())
        left = amps[...].reshape(8 * 64, deep)
        right = ints[...].reshape(deep, width)
        total = jnp.dot(left, right, preferred_element_type=F32) * keep
        total = jnp.where(row < live_shards(h) * 64, total, 0.0)
        total = total.reshape(8, 8, 8, width)
        for i in range(8):
            made_ref[i, pl.ds(h * 8, 8)] = total[:, i].astype(BF16)
        shards = pl.ds(h * 8, 8)
        pltpu.make_async_copy(made_ref.at[:, shards], out_ref.at[:, shards], out_sem).start()

    pltpu.make_async_copy(made_ref, out_ref, out_sem).wait()


def cycle_sum(count, pair, amps, int_own, int_other, keep):
    width = int_own.shape[3]
    return pl.pallas_call(
        cycle_kernel,
        out_shape=jax.ShapeDtypeStruct((8, SHARDS, 8, width), BF16),
        in_specs=[SCALARS, SCALARS] + [ANYWHERE] * 3 + [LOCAL],
        out_specs=ANYWHERE,
        scratch_shapes=[
            pltpu.VMEM((SHARDS, 64, OJ * VH), BF16),
            pltpu.VMEM((OJ, 8, VH, width), BF16),
            pltpu.VMEM((8, SHARDS, 8, width), BF16),
            pltpu.SemaphoreType.DMA((8,)),
            pltpu.SemaphoreType.DMA((8,)),
            pltpu.SemaphoreType.DMA,
        ],
        compiler_params=pltpu.CompilerParams(vmem_limit_bytes=60 << 20),
        cost_estimate=pl.CostEstimate(
            flops=2 * 4096 * 2048 * 256, bytes_accessed=27 << 20, transcendentals=0
        ),
    )(count, pair, amps, int_own, int_other, keep)


def body(amplitudes, integrals, cycle_integrals, virt_count):
    slot_width = VH
    ab_count = integrals.shape[0]
    cd_count = integrals.shape[1]
    jb_count = cycle_integrals.shape[1]
    pair = lax.axis_index("pair")
    virt = lax.axis_index("virt")
    pair_id = pair.astype(jnp.int32).reshape(1)
    cycle_other = lax.ppermute(cycle_integrals, "pair", SWAP)
    widths = [cd_count * n // 16 for n in range(7, 17)]

    def ladder_of(width):
        def sums(count, amplitudes, integrals):
            packed = pack_amps(count, pair_id, amplitudes, width)
            amps = lax.all_gather(packed, "virt", axis=0, tiled=True)
            weights = pack_weights(count, pair_id, integrals, width)
            return ladder_sums(pair_id, amps, weights)

        return sums

    tiles = live_tiles(virt_count).reshape(2, -1).sum(axis=1).max()
    choice = sum((tiles * 128 > width).astype(jnp.int32) for width in widths[:-1])
    own, sent = lax.switch(
        choice, [ladder_of(width) for width in widths], virt_count, amplitudes, integrals
    )
    keep_pairs = pair_mask(virt_count, virt * ab_count, ab_count, slot_width)[None, :]
    other = lax.ppermute(sent, "pair", SWAP)
    ladder_own, turned = combine(own, other, keep_pairs)
    amps = lax.all_gather(turned, "virt", axis=0, tiled=True).reshape(SHARDS, 64, OJ * VH)
    ladder_other = lax.ppermute(ladder_own, "pair", SWAP)
    ladder = jnp.concatenate(
        [
            jnp.where(pair == 0, ladder_own, ladder_other),
            jnp.where(pair == 0, ladder_other, ladder_own),
        ],
        axis=0,
    )
    keep_cols = slot_mask(virt_count, virt * jb_count, jb_count, slot_width)[None, :]
    shape4 = (16, 8, slot_width, jb_count)
    cycle = cycle_sum(
        virt_count,
        pair_id,
        amps,
        cycle_integrals.reshape(shape4),
        cycle_other.reshape(shape4),
        keep_cols,
    )
    return (ladder, cycle.reshape(8 * SHARDS * 8, jb_count))


def solution(mesh):
    placed = (P("virt", "pair"), P("virt", "pair"), P("pair", "virt"), P())
    return jax.shard_map(
        body,
        mesh=mesh,
        in_specs=placed,
        out_specs=(P(None, "virt"), P("pair", "virt")),
        check_vma=False,
    )
```

```python
import jax
import jax.numpy as jnp
from jax import lax
from jax.experimental import pallas as pl
from jax.experimental.pallas import tpu as pltpu
from jax.sharding import PartitionSpec as P

VH = 64
OI = 16
OJ = 32
F32 = jnp.float32
BF16 = jnp.bfloat16


def irrep_sizes(virt_count, irrep_of):
    irrep_ids = jnp.arange(virt_count.shape[0], dtype=jnp.int32)
    return jnp.sum(
        jnp.where(irrep_of[:, None] == irrep_ids[None, :], virt_count[None, :], 0), axis=1
    )


def pair_mask(virt_count, first_pos, length, slot_width):
    position = first_pos + jnp.arange(length, dtype=jnp.int32)
    irrep_of = position // (slot_width * slot_width)
    slot_one = position // slot_width % slot_width
    slot_two = position % slot_width
    irrep_size = irrep_sizes(virt_count, irrep_of)
    return ((slot_one < irrep_size) & (slot_two < irrep_size)).astype(F32)


def slot_mask(virt_count, first_pos, length, slot_width):
    position = (first_pos + jnp.arange(length, dtype=jnp.int32)) % (
        virt_count.shape[0] * slot_width
    )
    irrep_of = position // slot_width
    slot_ids = position % slot_width
    return (slot_ids < irrep_sizes(virt_count, irrep_of)).astype(F32)


SHARDS = 64
SWAP = [(0, 1), (1, 0)]


ANYWHERE = pl.BlockSpec(memory_space=pl.ANY)
SCALARS = pl.BlockSpec(memory_space=pltpu.SMEM)
LOCAL = pl.BlockSpec(memory_space=pltpu.VMEM)


NT = (((1,), (1,)), ((), ()))
STEPS = 8


def ladder_kernel(
    pair_ref, amp_ref, weight_ref, own_ref, sent_ref, held_ref, held_weight_ref, total_ref, sems
):
    depth = held_ref.shape[1] // STEPS

    def part(step):
        return pl.ds(pl.multiple_of(step * depth, 128), depth)

    def fetches(step):
        return [
            pltpu.make_async_copy(source.at[:, part(step)], held.at[:, part(step)], sems.at[n, step])
            for n, (source, held) in enumerate(((amp_ref, held_ref), (weight_ref, held_weight_ref)))
        ]

    for step in range(STEPS):
        for copy in fetches(step):
            copy.start()
    total_ref[...] = jnp.zeros_like(total_ref)

    @pl.loop(0, STEPS)
    def _(step):
        for copy in fetches(step):
            copy.wait()
        total_ref[...] += lax.dot_general(
            held_ref[:, part(step)], held_weight_ref[:, part(step)], NT, preferred_element_type=F32
        )

    half = own_ref.shape[0]
    own_ref[...] = total_ref[pl.ds(pl.multiple_of(pair_ref[0] * half, half), half)]
    sent_ref[...] = total_ref[pl.ds(pl.multiple_of((1 - pair_ref[0]) * half, half), half)]


def live_tiles(count):
    return (count * count + 127) >> 7


def pack_amps_kernel(count_ref, pair_ref, amp_ref, out_ref, wide_ref, all_ref, *part_refs):
    irreps = 4
    tiles = VH * VH // 128
    rows = amp_ref.shape[0]
    lane = lax.broadcasted_iota(jnp.int32, (rows, 128), 1)
    wide_ref[...] = amp_ref[...].astype(F32)
    for part_ref in part_refs:
        part_ref[...] = jnp.zeros_like(part_ref)
    counts = [count_ref[pair_ref[0] * irreps + h] for h in range(irreps)]

    @pl.loop(0, VH // 2, unroll=4)
    def _(row):
        todo = []
        for h in range(irreps):
            source = wide_ref[:, pl.ds(pl.multiple_of((h * tiles + row) * 128, 128), 128)]
            for odd in range(2):
                slot = 2 * row + odd
                first = slot * counts[h]
                place = first & 127
                turned = pltpu.roll(source, (place + 128 - VH * odd) & 127, 1)
                size = jnp.where(slot < counts[h], counts[h], 0)
                tile = jnp.minimum(first >> 7, tiles - 1)
                todo.append((h, tile, place, size, turned))
        for h, tile, place, size, turned in todo:
            here = part_refs[h].at[:, pl.ds(pl.multiple_of(tile * 128, 128), 128)]
            here[...] = jnp.where((lane >= place) & (lane < place + size), turned, here[...])
            after = part_refs[h].at[:, pl.ds(pl.multiple_of(tile * 128 + 128, 128), 128)]
            after[...] = jnp.where(lane < place + size - 128, turned, after[...])

    all_ref[...] = jnp.zeros_like(all_ref)
    tile = jnp.int32(0)
    for h in range(irreps):
        all_ref[:, pl.ds(pl.multiple_of(tile * 128, 128), VH * VH)] = part_refs[h][:, : VH * VH]
        tile += live_tiles(counts[h])
    out_ref[...] = all_ref[:, : out_ref.shape[1]].astype(BF16)


def pack_amps(count, pair, amps, width):
    rows, cols = amps.shape
    return pl.pallas_call(
        pack_amps_kernel,
        out_shape=jax.ShapeDtypeStruct((rows, width), BF16),
        in_specs=[SCALARS, SCALARS, LOCAL],
        out_specs=LOCAL,
        scratch_shapes=[
            pltpu.VMEM((rows, cols), F32),
            pltpu.VMEM((rows, cols + VH * VH), F32),
        ]
        + [pltpu.VMEM((rows, VH * VH + 128), F32)] * 4,
        cost_estimate=pl.CostEstimate(
            flops=32 * rows * cols, bytes_accessed=4 * rows * cols, transcendentals=0
        ),
    )(count, pair, amps)


WINDOW = 6 * VH


def pack_weights_kernel(count_ref, pair_ref, weight_ref, out_ref):
    irreps = 4
    irrep = pl.program_id(0)
    count = count_ref[pair_ref[0] * irreps + irrep]
    first = jnp.int32(0)
    for h in range(irreps - 1):
        first += jnp.where(h < irrep, live_tiles(count_ref[pair_ref[0] * irreps + h]), 0)
    row = lax.broadcasted_iota(jnp.int32, (WINDOW, 128), 0)
    column = lax.broadcasted_iota(jnp.int32, (WINDOW, 128), 1)
    wide_count = count.astype(F32)

    def put(tile, value):
        out_ref[:, pl.ds(pl.multiple_of(tile * 128, 128), 128)] = value

    @pl.loop(0, live_tiles(count))
    def _(tile):
        place = tile * 128 + column
        slot = jnp.floor((place.astype(F32) + 0.5) / wide_count).astype(jnp.int32)
        slot_first = (tile * 128) // count
        base = jnp.minimum(slot_first // 2 * 2, VH - 6)
        found = (slot - base) * VH + place - slot * count
        chosen = ((row == found) & (place < count * count)).astype(F32).astype(BF16)
        window = weight_ref[:, pl.ds(pl.multiple_of(base * VH, 128), WINDOW)]
        put(first + tile, jnp.dot(window, chosen, preferred_element_type=F32).astype(BF16))

    @pl.when(irrep == irreps - 1)
    def _():
        @pl.loop(first + live_tiles(count), out_ref.shape[1] // 128)
        def _(tile):
            put(tile, jnp.zeros((out_ref.shape[0], 128), BF16))


def pack_weights(count, pair, weights, width):
    rows, cols = weights.shape
    grid_spec = pltpu.PrefetchScalarGridSpec(
        num_scalar_prefetch=2,
        grid=(4,),
        in_specs=[pl.BlockSpec((rows, VH * VH), lambda h, c, p: (0, h))],
        out_specs=pl.BlockSpec((rows, width), lambda h, c, p: (0, 0)),
    )
    return pl.pallas_call(
        pack_weights_kernel,
        out_shape=jax.ShapeDtypeStruct((rows, width), BF16),
        grid_spec=grid_spec,
        compiler_params=pltpu.CompilerParams(
            dimension_semantics=("arbitrary",), vmem_limit_bytes=58 << 20
        ),
        cost_estimate=pl.CostEstimate(
            flops=2 * rows * cols * WINDOW, bytes_accessed=4 * rows * cols, transcendentals=0
        ),
    )(count, pair, weights)


def ladder_sums(pair, amps, integrals):
    rows, depth = amps.shape
    cols = integrals.shape[0]
    half = jax.ShapeDtypeStruct((rows // 2, cols), F32)
    return pl.pallas_call(
        ladder_kernel,
        out_shape=[half, half],
        in_specs=[SCALARS, ANYWHERE, ANYWHERE],
        out_specs=[LOCAL, LOCAL],
        scratch_shapes=[
            pltpu.VMEM((rows, depth), BF16),
            pltpu.VMEM((cols, depth), BF16),
            pltpu.VMEM((rows, cols), F32),
            pltpu.SemaphoreType.DMA((2, STEPS)),
        ],
        compiler_params=pltpu.CompilerParams(vmem_limit_bytes=60 << 20),
        cost_estimate=pl.CostEstimate(
            flops=2 * rows * cols * depth, bytes_accessed=36 << 20, transcendentals=0
        ),
    )(pair, amps, integrals)


def combine_kernel(own_ref, other_ref, keep_ref, ladder_ref, *refs):
    turned_ref, rows_ref, turn_ref = refs
    i_count = 8
    total = (own_ref[...] + other_ref[...]) * keep_ref[...]
    rounded = total.astype(BF16)
    ladder_ref[...] = rounded
    wide = rounded.astype(F32)
    for lane in range(4):
        rows_ref[lane] = wide[:, lane * 128 : (lane + 1) * 128]
    for kk in range(OJ // 2):
        for lane in range(4):
            even = rows_ref[lane, pl.ds(2 * kk, i_count, stride=OJ), :]
            odd = rows_ref[lane, pl.ds(2 * kk + 1, i_count, stride=OJ), :]
            turn_ref[kk, (2 * lane) * 8 : (2 * lane) * 8 + 8, :] = jnp.concatenate(
                [even[:, :VH], odd[:, :VH]], axis=1
            )
            turn_ref[kk, (2 * lane + 1) * 8 : (2 * lane + 1) * 8 + 8, :] = jnp.concatenate(
                [even[:, VH:], odd[:, VH:]], axis=1
            )
    for kk in range(OJ // 2):
        for i in range(i_count):
            turned_ref[i * 8 : i * 8 + 8, kk * 128 : (kk + 1) * 128] = turn_ref[
                kk, pl.ds(i, 8, stride=8), :
            ].astype(BF16)


def combine(own, other, keep):
    rows, cols = own.shape
    return pl.pallas_call(
        combine_kernel,
        out_shape=[jax.ShapeDtypeStruct((rows, cols), BF16)]
        + [jax.ShapeDtypeStruct((64, OJ * VH), BF16)],
        in_specs=[LOCAL] * 3,
        out_specs=[LOCAL] * 2,
        scratch_shapes=[
            pltpu.VMEM((4, rows, 128), F32),
            pltpu.VMEM((OJ // 2, rows * cols // (OJ * VH), 128), F32),
        ],
        compiler_params=pltpu.CompilerParams(vmem_limit_bytes=8 << 20),
        cost_estimate=pl.CostEstimate(
            flops=4 * rows * cols, bytes_accessed=12 * rows * cols, transcendentals=0
        ),
    )(own, other, keep)


def fetch_integrals(h, pair, int_own_ref, int_other_ref, int_ref, int_sem):
    for part, source in enumerate((int_own_ref, int_other_ref)):
        first = (pair if part == 0 else 1 - pair) * 16
        pltpu.make_async_copy(
            source.at[:, pl.ds(h, 1)],
            int_ref.at[pl.ds(first, 16), pl.ds(h, 1)],
            int_sem.at[h],
        ).start()


def cycle_kernel(count_ref, pair_ref, amps_ref, int_own_ref, int_other_ref, keep_ref, out_ref, *scratch):
    amp_ref, int_ref, made_ref, amp_sem, int_sem, out_sem = scratch
    keep = keep_ref[...]
    width = keep.shape[1]
    deep = OJ * VH

    def live_shards(h):
        return jnp.clip((count_ref[h] + 7) >> 3, 4, 8)

    def amps_copy(h, do):
        live = live_shards(h)
        for size in range(4, 9):

            @pl.when(live == size)
            def _(size=size):
                shards = pl.ds(h * 8, size)
                do(pltpu.make_async_copy(amps_ref.at[shards], amp_ref.at[shards], amp_sem.at[h]))

    def fetch(h):
        fetch_integrals(h, pair_ref[0], int_own_ref, int_other_ref, int_ref, int_sem)
        amps_copy(h, lambda copy: copy.start())

    row = lax.broadcasted_iota(jnp.int32, (8 * 64, width), 0)
    @pl.loop(0, 8)
    def _(h):
        fetch(h)

    @pl.loop(0, 8)
    def _(h):
        ints = int_ref.at[:, pl.ds(h, 1)]
        amps = amp_ref.at[pl.ds(h * 8, 8)]
        pltpu.make_async_copy(ints, ints, int_sem.at[h]).wait()
        amps_copy(h, lambda copy: copy.wait())
        left = amps[...].reshape(8 * 64, deep)
        right = ints[...].reshape(deep, width)
        total = jnp.dot(left, right, preferred_element_type=F32) * keep
        total = jnp.where(row < live_shards(h) * 64, total, 0.0)
        total = total.reshape(8, 8, 8, width)
        for i in range(8):
            made_ref[i, pl.ds(h * 8, 8)] = total[:, i].astype(BF16)
        shards = pl.ds(h * 8, 8)
        pltpu.make_async_copy(made_ref.at[:, shards], out_ref.at[:, shards], out_sem).start()

    pltpu.make_async_copy(made_ref, out_ref, out_sem).wait()


def cycle_sum(count, pair, amps, int_own, int_other, keep):
    width = int_own.shape[3]
    return pl.pallas_call(
        cycle_kernel,
        out_shape=jax.ShapeDtypeStruct((8, SHARDS, 8, width), BF16),
        in_specs=[SCALARS, SCALARS] + [ANYWHERE] * 3 + [LOCAL],
        out_specs=ANYWHERE,
        scratch_shapes=[
            pltpu.VMEM((SHARDS, 64, OJ * VH), BF16),
            pltpu.VMEM((OJ, 8, VH, width), BF16),
            pltpu.VMEM((8, SHARDS, 8, width), BF16),
            pltpu.SemaphoreType.DMA((8,)),
            pltpu.SemaphoreType.DMA((8,)),
            pltpu.SemaphoreType.DMA,
        ],
        compiler_params=pltpu.CompilerParams(vmem_limit_bytes=60 << 20),
        cost_estimate=pl.CostEstimate(
            flops=2 * 4096 * 2048 * 256, bytes_accessed=27 << 20, transcendentals=0
        ),
    )(count, pair, amps, int_own, int_other, keep)


def body(amplitudes, integrals, cycle_integrals, virt_count):
    slot_width = VH
    ab_count = integrals.shape[0]
    cd_count = integrals.shape[1]
    jb_count = cycle_integrals.shape[1]
    pair = lax.axis_index("pair")
    virt = lax.axis_index("virt")
    pair_id = pair.astype(jnp.int32).reshape(1)
    cycle_other = lax.ppermute(cycle_integrals, "pair", SWAP)
    widths = [cd_count * n // 16 for n in range(7, 17)]

    def ladder_of(width):
        def sums(count, amplitudes, integrals):
            packed = pack_amps(count, pair_id, amplitudes, width)
            amps = lax.all_gather(packed, "virt", axis=0, tiled=True)
            weights = pack_weights(count, pair_id, integrals, width)
            return ladder_sums(pair_id, amps, weights)

        return sums

    tiles = live_tiles(virt_count).reshape(2, -1).sum(axis=1).max()
    choice = sum((tiles * 128 > width).astype(jnp.int32) for width in widths[:-1])
    own, sent = lax.switch(
        choice, [ladder_of(width) for width in widths], virt_count, amplitudes, integrals
    )
    keep_pairs = pair_mask(virt_count, virt * ab_count, ab_count, slot_width)[None, :]
    other = lax.ppermute(sent, "pair", SWAP)
    ladder_own, turned = combine(own, other, keep_pairs)
    amps = lax.all_gather(turned, "virt", axis=0, tiled=True).reshape(SHARDS, 64, OJ * VH)
    ladder_other = lax.ppermute(ladder_own, "pair", SWAP)
    ladder = jnp.concatenate(
        [
            jnp.where(pair == 0, ladder_own, ladder_other),
            jnp.where(pair == 0, ladder_other, ladder_own),
        ],
        axis=0,
    )
    keep_cols = slot_mask(virt_count, virt * jb_count, jb_count, slot_width)[None, :]
    shape4 = (16, 8, slot_width, jb_count)
    cycle = cycle_sum(
        virt_count,
        pair_id,
        amps,
        cycle_integrals.reshape(shape4),
        cycle_other.reshape(shape4),
        keep_cols,
    )
    return (ladder, cycle.reshape(8 * SHARDS * 8, jb_count))


def solution(mesh):
    placed = (P("virt", "pair"), P("virt", "pair"), P("pair", "virt"), P())
    return jax.shard_map(
        body,
        mesh=mesh,
        in_specs=placed,
        out_specs=(P(None, "virt"), P("pair", "virt")),
        check_vma=False,
    )
```

```python
import jax
import jax.numpy as jnp
from jax import lax
from jax.experimental import pallas as pl
from jax.experimental.pallas import tpu as pltpu
from jax.sharding import PartitionSpec as P

VH = 64
OI = 16
OJ = 32
F32 = jnp.float32
BF16 = jnp.bfloat16


def irrep_sizes(virt_count, irrep_of):
    irrep_ids = jnp.arange(virt_count.shape[0], dtype=jnp.int32)
    return jnp.sum(
        jnp.where(irrep_of[:, None] == irrep_ids[None, :], virt_count[None, :], 0), axis=1
    )


def pair_mask(virt_count, first_pos, length, slot_width):
    position = first_pos + jnp.arange(length, dtype=jnp.int32)
    irrep_of = position // (slot_width * slot_width)
    slot_one = position // slot_width % slot_width
    slot_two = position % slot_width
    irrep_size = irrep_sizes(virt_count, irrep_of)
    return ((slot_one < irrep_size) & (slot_two < irrep_size)).astype(F32)


def slot_mask(virt_count, first_pos, length, slot_width):
    position = (first_pos + jnp.arange(length, dtype=jnp.int32)) % (
        virt_count.shape[0] * slot_width
    )
    irrep_of = position // slot_width
    slot_ids = position % slot_width
    return (slot_ids < irrep_sizes(virt_count, irrep_of)).astype(F32)


SHARDS = 64
SWAP = [(0, 1), (1, 0)]


ANYWHERE = pl.BlockSpec(memory_space=pl.ANY)
SCALARS = pl.BlockSpec(memory_space=pltpu.SMEM)
LOCAL = pl.BlockSpec(memory_space=pltpu.VMEM)


NT = (((1,), (1,)), ((), ()))
STEPS = 8


def ladder_kernel(
    pair_ref, amp_ref, weight_ref, own_ref, sent_ref, held_ref, held_weight_ref, total_ref, sems
):
    depth = held_ref.shape[1] // STEPS

    def part(step):
        return pl.ds(pl.multiple_of(step * depth, 128), depth)

    def fetches(step):
        return [
            pltpu.make_async_copy(source.at[:, part(step)], held.at[:, part(step)], sems.at[n, step])
            for n, (source, held) in enumerate(((amp_ref, held_ref), (weight_ref, held_weight_ref)))
        ]

    for step in range(STEPS):
        for copy in fetches(step):
            copy.start()
    total_ref[...] = jnp.zeros_like(total_ref)

    @pl.loop(0, STEPS)
    def _(step):
        for copy in fetches(step):
            copy.wait()
        total_ref[...] += lax.dot_general(
            held_ref[:, part(step)], held_weight_ref[:, part(step)], NT, preferred_element_type=F32
        )

    half = own_ref.shape[0]
    own_ref[...] = total_ref[pl.ds(pl.multiple_of(pair_ref[0] * half, half), half)]
    sent_ref[...] = total_ref[pl.ds(pl.multiple_of((1 - pair_ref[0]) * half, half), half)]


def live_tiles(count):
    return (count * count + 127) >> 7


def pack_amps_kernel(count_ref, pair_ref, amp_ref, out_ref, wide_ref, all_ref, *part_refs):
    irreps = 4
    tiles = VH * VH // 128
    rows = amp_ref.shape[0]
    lane = lax.broadcasted_iota(jnp.int32, (rows, 128), 1)
    wide_ref[...] = amp_ref[...].astype(F32)
    for part_ref in part_refs:
        part_ref[...] = jnp.zeros_like(part_ref)
    counts = [count_ref[pair_ref[0] * irreps + h] for h in range(irreps)]

    @pl.loop(0, VH // 2, unroll=8)
    def _(row):
        todo = []
        for h in range(irreps):
            source = wide_ref[:, pl.ds(pl.multiple_of((h * tiles + row) * 128, 128), 128)]
            for odd in range(2):
                slot = 2 * row + odd
                first = slot * counts[h]
                place = first & 127
                turned = pltpu.roll(source, (place + 128 - VH * odd) & 127, 1)
                size = jnp.where(slot < counts[h], counts[h], 0)
                tile = jnp.minimum(first >> 7, tiles - 1)
                todo.append((h, tile, place, size, turned))
        for h, tile, place, size, turned in todo:
            here = part_refs[h].at[:, pl.ds(pl.multiple_of(tile * 128, 128), 128)]
            here[...] = jnp.where((lane >= place) & (lane < place + size), turned, here[...])
            after = part_refs[h].at[:, pl.ds(pl.multiple_of(tile * 128 + 128, 128), 128)]
            after[...] = jnp.where(lane < place + size - 128, turned, after[...])

    all_ref[...] = jnp.zeros_like(all_ref)
    tile = jnp.int32(0)
    for h in range(irreps):
        all_ref[:, pl.ds(pl.multiple_of(tile * 128, 128), VH * VH)] = part_refs[h][:, : VH * VH]
        tile += live_tiles(counts[h])
    out_ref[...] = all_ref[:, : out_ref.shape[1]].astype(BF16)


def pack_amps(count, pair, amps, width):
    rows, cols = amps.shape
    return pl.pallas_call(
        pack_amps_kernel,
        out_shape=jax.ShapeDtypeStruct((rows, width), BF16),
        in_specs=[SCALARS, SCALARS, LOCAL],
        out_specs=LOCAL,
        scratch_shapes=[
            pltpu.VMEM((rows, cols), F32),
            pltpu.VMEM((rows, cols + VH * VH), F32),
        ]
        + [pltpu.VMEM((rows, VH * VH + 128), F32)] * 4,
        cost_estimate=pl.CostEstimate(
            flops=32 * rows * cols, bytes_accessed=4 * rows * cols, transcendentals=0
        ),
    )(count, pair, amps)


WINDOW = 6 * VH


def pack_weights_kernel(count_ref, pair_ref, weight_ref, out_ref):
    irreps = 4
    irrep = pl.program_id(0)
    count = count_ref[pair_ref[0] * irreps + irrep]
    first = jnp.int32(0)
    for h in range(irreps - 1):
        first += jnp.where(h < irrep, live_tiles(count_ref[pair_ref[0] * irreps + h]), 0)
    row = lax.broadcasted_iota(jnp.int32, (WINDOW, 128), 0)
    column = lax.broadcasted_iota(jnp.int32, (WINDOW, 128), 1)
    wide_count = count.astype(F32)

    def put(tile, value):
        out_ref[:, pl.ds(pl.multiple_of(tile * 128, 128), 128)] = value

    @pl.loop(0, live_tiles(count))
    def _(tile):
        place = tile * 128 + column
        slot = jnp.floor((place.astype(F32) + 0.5) / wide_count).astype(jnp.int32)
        slot_first = (tile * 128) // count
        base = jnp.minimum(slot_first // 2 * 2, VH - 6)
        found = (slot - base) * VH + place - slot * count
        chosen = ((row == found) & (place < count * count)).astype(F32).astype(BF16)
        window = weight_ref[:, pl.ds(pl.multiple_of(base * VH, 128), WINDOW)]
        put(first + tile, jnp.dot(window, chosen, preferred_element_type=F32).astype(BF16))

    @pl.when(irrep == irreps - 1)
    def _():
        @pl.loop(first + live_tiles(count), out_ref.shape[1] // 128)
        def _(tile):
            put(tile, jnp.zeros((out_ref.shape[0], 128), BF16))


def pack_weights(count, pair, weights, width):
    rows, cols = weights.shape
    grid_spec = pltpu.PrefetchScalarGridSpec(
        num_scalar_prefetch=2,
        grid=(4,),
        in_specs=[pl.BlockSpec((rows, VH * VH), lambda h, c, p: (0, h))],
        out_specs=pl.BlockSpec((rows, width), lambda h, c, p: (0, 0)),
    )
    return pl.pallas_call(
        pack_weights_kernel,
        out_shape=jax.ShapeDtypeStruct((rows, width), BF16),
        grid_spec=grid_spec,
        compiler_params=pltpu.CompilerParams(
            dimension_semantics=("arbitrary",), vmem_limit_bytes=58 << 20
        ),
        cost_estimate=pl.CostEstimate(
            flops=2 * rows * cols * WINDOW, bytes_accessed=4 * rows * cols, transcendentals=0
        ),
    )(count, pair, weights)


def ladder_sums(pair, amps, integrals):
    rows, depth = amps.shape
    cols = integrals.shape[0]
    half = jax.ShapeDtypeStruct((rows // 2, cols), F32)
    return pl.pallas_call(
        ladder_kernel,
        out_shape=[half, half],
        in_specs=[SCALARS, ANYWHERE, ANYWHERE],
        out_specs=[LOCAL, LOCAL],
        scratch_shapes=[
            pltpu.VMEM((rows, depth), BF16),
            pltpu.VMEM((cols, depth), BF16),
            pltpu.VMEM((rows, cols), F32),
            pltpu.SemaphoreType.DMA((2, STEPS)),
        ],
        compiler_params=pltpu.CompilerParams(vmem_limit_bytes=60 << 20),
        cost_estimate=pl.CostEstimate(
            flops=2 * rows * cols * depth, bytes_accessed=36 << 20, transcendentals=0
        ),
    )(pair, amps, integrals)


def combine_kernel(own_ref, other_ref, keep_ref, ladder_ref, *refs):
    turned_ref, rows_ref, turn_ref = refs
    i_count = 8
    total = (own_ref[...] + other_ref[...]) * keep_ref[...]
    rounded = total.astype(BF16)
    ladder_ref[...] = rounded
    wide = rounded.astype(F32)
    for lane in range(4):
        rows_ref[lane] = wide[:, lane * 128 : (lane + 1) * 128]
    for kk in range(OJ // 2):
        for lane in range(4):
            even = rows_ref[lane, pl.ds(2 * kk, i_count, stride=OJ), :]
            odd = rows_ref[lane, pl.ds(2 * kk + 1, i_count, stride=OJ), :]
            turn_ref[kk, (2 * lane) * 8 : (2 * lane) * 8 + 8, :] = jnp.concatenate(
                [even[:, :VH], odd[:, :VH]], axis=1
            )
            turn_ref[kk, (2 * lane + 1) * 8 : (2 * lane + 1) * 8 + 8, :] = jnp.concatenate(
                [even[:, VH:], odd[:, VH:]], axis=1
            )
    for kk in range(OJ // 2):
        for i in range(i_count):
            turned_ref[i * 8 : i * 8 + 8, kk * 128 : (kk + 1) * 128] = turn_ref[
                kk, pl.ds(i, 8, stride=8), :
            ].astype(BF16)


def combine(own, other, keep):
    rows, cols = own.shape
    return pl.pallas_call(
        combine_kernel,
        out_shape=[jax.ShapeDtypeStruct((rows, cols), BF16)]
        + [jax.ShapeDtypeStruct((64, OJ * VH), BF16)],
        in_specs=[LOCAL] * 3,
        out_specs=[LOCAL] * 2,
        scratch_shapes=[
            pltpu.VMEM((4, rows, 128), F32),
            pltpu.VMEM((OJ // 2, rows * cols // (OJ * VH), 128), F32),
        ],
        compiler_params=pltpu.CompilerParams(vmem_limit_bytes=8 << 20),
        cost_estimate=pl.CostEstimate(
            flops=4 * rows * cols, bytes_accessed=12 * rows * cols, transcendentals=0
        ),
    )(own, other, keep)


def fetch_integrals(h, pair, int_own_ref, int_other_ref, int_ref, int_sem):
    for part, source in enumerate((int_own_ref, int_other_ref)):
        first = (pair if part == 0 else 1 - pair) * 16
        pltpu.make_async_copy(
            source.at[:, pl.ds(h, 1)],
            int_ref.at[pl.ds(first, 16), pl.ds(h, 1)],
            int_sem.at[h],
        ).start()


def cycle_kernel(count_ref, pair_ref, amps_ref, int_own_ref, int_other_ref, keep_ref, out_ref, *scratch):
    amp_ref, int_ref, made_ref, amp_sem, int_sem, out_sem = scratch
    keep = keep_ref[...]
    width = keep.shape[1]
    deep = OJ * VH

    def live_shards(h):
        return jnp.clip((count_ref[h] + 7) >> 3, 4, 8)

    def amps_copy(h, do):
        live = live_shards(h)
        for size in range(4, 9):

            @pl.when(live == size)
            def _(size=size):
                shards = pl.ds(h * 8, size)
                do(pltpu.make_async_copy(amps_ref.at[shards], amp_ref.at[shards], amp_sem.at[h]))

    def fetch(h):
        fetch_integrals(h, pair_ref[0], int_own_ref, int_other_ref, int_ref, int_sem)
        amps_copy(h, lambda copy: copy.start())

    row = lax.broadcasted_iota(jnp.int32, (8 * 64, width), 0)
    @pl.loop(0, 8)
    def _(h):
        fetch(h)

    @pl.loop(0, 8)
    def _(h):
        ints = int_ref.at[:, pl.ds(h, 1)]
        amps = amp_ref.at[pl.ds(h * 8, 8)]
        pltpu.make_async_copy(ints, ints, int_sem.at[h]).wait()
        amps_copy(h, lambda copy: copy.wait())
        left = amps[...].reshape(8 * 64, deep)
        right = ints[...].reshape(deep, width)
        total = jnp.dot(left, right, preferred_element_type=F32) * keep
        total = jnp.where(row < live_shards(h) * 64, total, 0.0)
        total = total.reshape(8, 8, 8, width)
        for i in range(8):
            made_ref[i, pl.ds(h * 8, 8)] = total[:, i].astype(BF16)
        shards = pl.ds(h * 8, 8)
        pltpu.make_async_copy(made_ref.at[:, shards], out_ref.at[:, shards], out_sem).start()

    pltpu.make_async_copy(made_ref, out_ref, out_sem).wait()


def cycle_sum(count, pair, amps, int_own, int_other, keep):
    width = int_own.shape[3]
    return pl.pallas_call(
        cycle_kernel,
        out_shape=jax.ShapeDtypeStruct((8, SHARDS, 8, width), BF16),
        in_specs=[SCALARS, SCALARS] + [ANYWHERE] * 3 + [LOCAL],
        out_specs=ANYWHERE,
        scratch_shapes=[
            pltpu.VMEM((SHARDS, 64, OJ * VH), BF16),
            pltpu.VMEM((OJ, 8, VH, width), BF16),
            pltpu.VMEM((8, SHARDS, 8, width), BF16),
            pltpu.SemaphoreType.DMA((8,)),
            pltpu.SemaphoreType.DMA((8,)),
            pltpu.SemaphoreType.DMA,
        ],
        compiler_params=pltpu.CompilerParams(vmem_limit_bytes=60 << 20),
        cost_estimate=pl.CostEstimate(
            flops=2 * 4096 * 2048 * 256, bytes_accessed=27 << 20, transcendentals=0
        ),
    )(count, pair, amps, int_own, int_other, keep)


def body(amplitudes, integrals, cycle_integrals, virt_count):
    slot_width = VH
    ab_count = integrals.shape[0]
    cd_count = integrals.shape[1]
    jb_count = cycle_integrals.shape[1]
    pair = lax.axis_index("pair")
    virt = lax.axis_index("virt")
    pair_id = pair.astype(jnp.int32).reshape(1)
    cycle_other = lax.ppermute(cycle_integrals, "pair", SWAP)
    widths = [cd_count * n // 16 for n in range(7, 17)]

    def ladder_of(width):
        def sums(count, amplitudes, integrals):
            packed = pack_amps(count, pair_id, amplitudes, width)
            amps = lax.all_gather(packed, "virt", axis=0, tiled=True)
            weights = pack_weights(count, pair_id, integrals, width)
            return ladder_sums(pair_id, amps, weights)

        return sums

    tiles = live_tiles(virt_count)
    low = jnp.arange(tiles.shape[0], dtype=jnp.int32) < tiles.shape[0] // 2
    tiles = jnp.maximum(jnp.sum(jnp.where(low, tiles, 0)), jnp.sum(jnp.where(low, 0, tiles)))
    choice = sum((tiles * 128 > width).astype(jnp.int32) for width in widths[:-1])
    own, sent = lax.switch(
        choice, [ladder_of(width) for width in widths], virt_count, amplitudes, integrals
    )
    keep_pairs = pair_mask(virt_count, virt * ab_count, ab_count, slot_width)[None, :]
    other = lax.ppermute(sent, "pair", SWAP)
    ladder_own, turned = combine(own, other, keep_pairs)
    amps = lax.all_gather(turned, "virt", axis=0, tiled=True).reshape(SHARDS, 64, OJ * VH)
    ladder_other = lax.ppermute(ladder_own, "pair", SWAP)
    ladder = jnp.concatenate(
        [
            jnp.where(pair == 0, ladder_own, ladder_other),
            jnp.where(pair == 0, ladder_other, ladder_own),
        ],
        axis=0,
    )
    keep_cols = slot_mask(virt_count, virt * jb_count, jb_count, slot_width)[None, :]
    shape4 = (16, 8, slot_width, jb_count)
    cycle = cycle_sum(
        virt_count,
        pair_id,
        amps,
        cycle_integrals.reshape(shape4),
        cycle_other.reshape(shape4),
        keep_cols,
    )
    return (ladder, cycle.reshape(8 * SHARDS * 8, jb_count))


def solution(mesh):
    placed = (P("virt", "pair"), P("virt", "pair"), P("pair", "virt"), P())
    return jax.shard_map(
        body,
        mesh=mesh,
        in_specs=placed,
        out_specs=(P(None, "virt"), P("pair", "virt")),
        check_vma=False,
    )
```
